32 devices in a mesh: pair: 16 (over z, y, x), sum: 2 (over core).
Axes of the slice: x: 2, y: 2, z: 4, core: 2. Of those that a mesh axis runs over, the one named last changes fastest.
Arguments:
- amps: bfloat16 [128, 2, 12288], P('pair', 'sum'), may hold values from -6 to 6
- amp_mask: int32 [2, 192], P('sum'), may hold values 0 or 1
- hh_ints: bfloat16 [128, 128], P('pair'), may hold values from -0.5 to 0.5
- integrals: bfloat16 [16, 2, 384, 4096], P('pair', 'sum'), may hold values from -0.25 to 0.25
- slot_info: int32 [16, 2, 24, 16], P('pair', 'sum'), may hold values from 0 to 31, as said below
- slot_count: int32 [16, 2, 24], P('pair', 'sum'), may hold values from 1 to 16, as said below
- need_tiles: int32 [16, 2, 32], P(None, 'sum'), may hold values from 0 to 191, as said below
- slab_pairs: int32 [128, 2], replicated, may hold values from 0 to 199
- occ_energy: float32 [200], replicated, may hold values from -1.5 to -0.5
- virt_energy: float32 [1536], replicated, may hold values from 0.1 to 1.5
Outputs:
- residual: float32 [128, 2, 12288], P(None, 'sum', 'pair')
The draws below stay inside these ranges and needn't reach their ends.
Inputs may be any that keep to these rules, and one draw needn't show every extreme that they name: `slot_info`: the 16 positions listed for one owner tile are distinct; slot g of a tile is live when g is below its count. `slot_count`: some owner tile of the slice has all 16 slots live. `need_tiles`: no tile repeats within one owner's list.
All inputs are finite; a program needn't handle non-finite values. No bound on the sum of `amp_mask` on one device may be relied on, other than what follows from the above.
Results may differ from the reference program's by a relative error of at most 0.0015.
Values may be sent and summed in bfloat16 or wider, within the bound.
A program may use at most 128 MiB of HBM per device.

```python
import math
import jax
import jax.numpy as jnp
from jax import lax

NOCC = 200
NVIRT = 1536
TILE = 64
AS = 8
NEED = 32
G = 16
BT = 24
M = 128
SHARD = 12288
HC = 768
OWN = 24
N_PAIR = 16
N_SUM = 2


def first_picks(key, list_count, width, keep):
    keys = jax.random.split(key, list_count)
    orders = jax.vmap(lambda single: jax.random.permutation(single, width))(keys)
    return orders[:, :keep]


def force_top(lists, top_value):
    present = jnp.any(lists[0] == top_value)
    head_value = jnp.where(present, lists[0, 0], top_value)
    return lists.at[0, 0].set(head_value)


def draw_need_tiles(key, part):
    lists = first_picks(key, N_PAIR * N_SUM, AS * BT, NEED)
    lists = force_top(lists, AS * BT - 1)
    return lists.reshape(N_PAIR, N_SUM, NEED).astype(jnp.int32)


def draw_slot_info(key, part):
    lists = first_picks(jax.random.fold_in(key, 7), N_PAIR * N_SUM * OWN, NEED, G)
    lists = force_top(lists, NEED - 1)
    return lists.reshape(N_PAIR, N_SUM, OWN, G).astype(jnp.int32)


def draw_slot_count(key, part):
    key_device, key_tile, key_peak = jax.random.split(jax.random.fold_in(key, 11), 3)
    device_load = jax.random.randint(key_device, (N_PAIR * N_SUM, 1), 0, G)
    tile_load = jax.random.randint(key_tile, (N_PAIR * N_SUM, OWN), 0, G)
    counts = 1 + device_load * tile_load // G
    peak = jax.random.randint(key_peak, (), 0, N_PAIR * N_SUM * OWN)
    flat_counts = jnp.where(jnp.arange(N_PAIR * N_SUM * OWN) == peak, G, counts.reshape(N_PAIR * N_SUM * OWN))
    return flat_counts.reshape(N_PAIR, N_SUM, OWN).astype(jnp.int32)


def with_ends(values, rng, smallest, largest):
    place = [jax.random.randint(jax.random.fold_in(rng, axis), (), 0, length) for axis, length in enumerate(values.shape)]
    main_axis = values.shape.index(max(values.shape))
    next_to = place[:main_axis] + [(place[main_axis] + 1) % values.shape[main_axis]] + place[main_axis + 1:]
    return values.at[tuple(place)].set(smallest).at[tuple(next_to)].set(largest)


def block_scale(stream_key, shape, shards, least, largest):
    gain = 1.0
    for axis_at, shards_of in shards:
        heights = jax.random.uniform(jax.random.fold_in(jax.random.fold_in(stream_key, 6), axis_at), (shards_of,), jnp.float32, least / len(shards), largest / len(shards))
        gain = gain * jnp.repeat(jnp.exp(heights), shape[axis_at] // shards_of).reshape((-1,) + (1,) * (len(shape) - 1 - axis_at))
    return gain


def normal_values(own_key, shape, spread, bound, pieces=(), kind=jnp.bfloat16):
    loudness = block_scale(own_key, shape, pieces, -0.22, 0.18) if pieces else 1.0
    result = jax.random.normal(own_key, shape, jnp.float32) * spread * loudness
    return jnp.minimum(jnp.maximum(result, -bound), bound).astype(kind)


def setup_inputs(seed: int = 0) -> dict:
    arg_keys = jax.random.split(jax.random.key(seed), 11)
    amps = normal_values(arg_keys[0], (M, N_SUM, SHARD), 1.0, 6.0, ((0, 16), (1, 2)))
    amp_mask = with_ends((jax.random.randint(arg_keys[1], (N_SUM, AS * BT), 0, 4) < 3).astype(jnp.int32), jax.random.fold_in(arg_keys[1], 1), 0, 1)
    hh_ints = normal_values(arg_keys[2], (M, M), M ** -0.5, 0.5, ((0, 16),))
    integrals = normal_values(arg_keys[3], (N_PAIR, N_SUM, OWN * G, TILE * TILE), (N_SUM * TILE * (G // 4 + 1)) ** -0.5, 0.25, ((0, 16), (1, 2)))
    slot_info = draw_slot_info(jax.random.fold_in(arg_keys[10], 71), 0)
    slot_count = draw_slot_count(jax.random.fold_in(arg_keys[10], 71), 0)
    need_tiles = draw_need_tiles(jax.random.fold_in(arg_keys[10], 71), 0)
    slab_pairs = with_ends(jax.random.randint(arg_keys[7], (M, 2), 0, NOCC), jax.random.fold_in(arg_keys[7], 1), 0, NOCC - 1).astype(jnp.int32)
    occ_energy = jnp.clip(jax.random.uniform(arg_keys[8], (NOCC,), jnp.float32, -1.5, -0.5), -1.5, -0.5)
    virt_energy = jnp.clip(jnp.exp(jax.random.uniform(arg_keys[9], (NVIRT,), jnp.float32, math.log(0.1), math.log(1.5))), 0.1, 1.5)
    return dict(amps=amps, amp_mask=amp_mask, hh_ints=hh_ints, integrals=integrals, slot_info=slot_info, slot_count=slot_count, need_tiles=need_tiles, slab_pairs=slab_pairs, occ_energy=occ_energy, virt_energy=virt_energy)


def reference(amps, amp_mask, hh_ints, integrals, slot_info, slot_count, need_tiles, slab_pairs, occ_energy, virt_energy):
    shard_tiles = AS * BT
    mask_values = amp_mask.astype(jnp.bfloat16)
    masked = (amps.reshape(M, N_SUM, shard_tiles, TILE) * mask_values[None, :, :, None]).reshape(M, N_SUM, SHARD)
    columns = jnp.arange(SHARD, dtype=jnp.int32)
    first_orbital = jnp.arange(N_SUM, dtype=jnp.int32)[:, None] * AS + columns[None, :] // NVIRT
    second_orbital = columns % NVIRT
    pair_energy = virt_energy[first_orbital] + virt_energy[second_orbital][None, :]
    occ_pair = occ_energy[slab_pairs[:, 0]] + occ_energy[slab_pairs[:, 1]]
    energy = pair_energy[None, :, :] - occ_pair[:, None, None]
    hole_hole = jnp.dot(hh_ints, masked.reshape(M, N_SUM * SHARD), preferred_element_type=jnp.float32).reshape(M, N_SUM, SHARD)

    def owner_ladder(owner_index):
        ladder_sum = jnp.zeros((M, OWN * TILE), jnp.float32)
        for sum_index in range(N_SUM):
            tile_cols = masked[:, sum_index, :].reshape(M, shard_tiles, TILE)
            need_list = lax.dynamic_index_in_dim(need_tiles[:, sum_index, :], owner_index, 0, keepdims=False)
            picked = jnp.take(tile_cols, need_list, axis=1)
            positions = lax.dynamic_index_in_dim(slot_info[:, sum_index], owner_index, 0, keepdims=False)
            live_counts = lax.dynamic_index_in_dim(slot_count[:, sum_index], owner_index, 0, keepdims=False)
            weights = lax.dynamic_index_in_dim(integrals[:, sum_index], owner_index, 0, keepdims=False).reshape(OWN, G, TILE, TILE)
            live_mask = jnp.arange(G, dtype=jnp.int32)[None, :] < live_counts[:, None]
            weights = jnp.where(live_mask[:, :, None, None], weights, jnp.zeros((), jnp.bfloat16)).astype(jnp.float32)
            chosen = jnp.take(picked, positions.reshape(OWN * G), axis=1).reshape(M, OWN, G, TILE).astype(jnp.float32)
            ladder_part = jnp.einsum('mogx,ogxy->moy', chosen, weights).reshape(M, OWN * TILE)
            rounded = lax.optimization_barrier(ladder_part.astype(jnp.bfloat16))
            ladder_sum = ladder_sum + rounded.astype(jnp.float32)
        return ladder_sum

    owners = lax.map(owner_ladder, jnp.arange(N_PAIR, dtype=jnp.int32))
    ladder = owners.reshape(N_PAIR, M, N_SUM, HC).transpose(1, 2, 0, 3).reshape(M, N_SUM, SHARD)
    return energy * masked.astype(jnp.float32) + hole_hole + ladder
```

```python
import functools

import jax
import jax.numpy as jnp
from jax import lax
from jax.experimental import pallas as pl
from jax.experimental.pallas import tpu as pltpu
from jax.sharding import PartitionSpec as P

TILE = 64
LANES = 128
LAYERS = 4
SHARD_STEP = 1
MESH = pl.DeviceIdType.MESH
BF16 = jnp.bfloat16
F32 = jnp.float32
I32 = jnp.int32


def iota(shape, axis):
    return lax.broadcasted_iota(I32, shape, axis)


def ladder_kernel(
    dims,
    mask_in,
    need_in,
    amps_in,
    hh_in,
    info_in,
    count_in,
    slab_in,
    occ_in,
    virt_in,
    ints_in,
    out_ref,
    mask_ref,
    need_ref,
    amps_ref,
    hh_ref,
    info_ref,
    count_ref,
    slab_ref,
    occ_ref,
    virt_ref,
    pos_ref,
    plain,
    low,
    high,
    pattern,
    ints,
    weights,
    send,
    recv,
    left,
    part_send,
    part_recv,
    shard_ref,
    shard_hh,
    relay,
    ready,
    ready_sum,
    in_sems,
    send_sems,
    recv_sems,
    part_send_sems,
    part_recv_sems,
    shard_send_sems,
    shard_recv_sems,
    relay_sems,
):
    n_pair, n_sum, rows, chunks, need, group, home_tiles, quads = dims
    slab = rows * n_pair
    home_pad = quads * 256
    home_cols = home_tiles * TILE
    pick_cols = need * TILE
    me = lax.axis_index("pair")
    my_sum = lax.axis_index("sum")

    width = n_pair // LAYERS
    layer, column = me // width, lax.rem(me, width)
    flip = layer // 2
    at_end = layer == flip * (LAYERS - 1)
    partner = lax.rem(me + n_pair // 2, n_pair)

    barrier = pltpu.get_barrier_semaphore()

    def greet(peer, carry):
        pl.semaphore_signal(barrier, inc=1, device_id=(peer, my_sum), device_id_type=MESH)
        return carry

    def greet_sum(peer, carry):
        pl.semaphore_signal(barrier, inc=1, device_id=(me, peer), device_id_type=MESH)
        return carry

    lax.fori_loop(me + 1, n_pair, greet, 0)
    lax.fori_loop(my_sum + 1, n_sum, greet_sum, 0)

    pairs_of_refs = (
        (mask_in, mask_ref),
        (amps_in, amps_ref),
        (need_in, need_ref),
        (hh_in, hh_ref),
        (info_in, info_ref),
        (count_in, count_ref),
        (slab_in, slab_ref),
        (occ_in, occ_ref),
        (virt_in, virt_ref),
        (ints_in, ints),
    )
    fetches = [
        pltpu.make_async_copy(src, dst, in_sems.at[at]) for at, (src, dst) in enumerate(pairs_of_refs)
    ]
    for fetch in fetches:
        fetch.start()

    @pl.when(me + my_sum > 0)
    def _():
        pl.semaphore_wait(barrier, me + my_sum)

    def answer(peer, carry):
        @pl.when((peer >= width) | (flip == 0) | (peer == partner))
        def _():
            pl.semaphore_signal(
                ready.at[me], inc=1, device_id=(peer, my_sum), device_id_type=MESH
            )

        return carry

    def answer_sum(peer, carry):
        pl.semaphore_signal(
            ready_sum.at[my_sum], inc=1, device_id=(me, peer), device_id_type=MESH
        )
        return carry

    lax.fori_loop(0, me, answer, 0)
    lax.fori_loop(0, my_sum, answer_sum, 0)

    def wait_ready(peer):
        @pl.when(peer > me)
        def _():
            pl.semaphore_wait(ready.at[peer], 1)

    def shard_copies():
        return [
            pltpu.make_async_remote_copy(
                src_ref=src,
                dst_ref=dst,
                send_sem=shard_send_sems.at[at],
                recv_sem=shard_recv_sems.at[at],
                device_id=(partner, my_sum),
                device_id_type=MESH,
            )
            for at, (src, dst) in enumerate(((amps_in, shard_ref), (hh_in, shard_hh)))
        ]

    @pl.when(at_end & (flip == 1))
    def _():
        for copy in shard_copies():
            copy.start()

    fetches[0].wait()
    fetches[1].wait()

    low_half = iota((rows, LANES), 1) < TILE
    row_at = iota((LANES, LANES), 0)
    col_at = iota((LANES, LANES), 1)
    origin = (
        (col_at & 64) + (col_at & 32) + ((col_at & 15) << 1) + ((col_at >> 4) & 1)
    )
    shuffle = jnp.where(row_at == origin, 1.0, 0.0).astype(BF16)

    def unfold(which, source):
        for chunk in range(chunks):
            keep = jnp.where(low_half, mask_ref[0, 2 * chunk], mask_ref[0, 2 * chunk + 1]).astype(F32)
            values = source[:, chunk * LANES : (chunk + 1) * LANES].astype(F32)
            plain[which, chunk] = values * keep
        moved = jnp.dot(
            plain[which].reshape(chunks * rows, LANES).astype(BF16),
            shuffle,
            preferred_element_type=F32,
        )
        turned = pltpu.roll(moved, TILE, 1)
        moved = moved.reshape(chunks, rows, LANES)
        turned = turned.reshape(chunks, rows, LANES)
        low[which] = jnp.stack([moved, turned], axis=1).reshape(2 * chunks, rows, LANES)
        high[which] = jnp.stack([turned, moved], axis=1).reshape(2 * chunks, rows, LANES)

    unfold(0, amps_ref)

    fetches[2].wait()
    fetches[3].wait()

    def pack(which, peer, hh):
        pieces = []
        for at in range(need // 2):
            first = need_ref[peer, 2 * at]
            second = need_ref[peer, 2 * at + 1]
            pieces.append(jnp.where(low_half, low[which, first], high[which, second]))
        for at in range(home_pad // LANES):
            if home_tiles % 2 == 0:
                pieces.append(plain[which, peer * (home_tiles // 2) + at])
            else:
                first = peer * home_tiles + 2 * at
                odd = lax.rem(first, 2)
                chunk = first // 2
                after = jnp.minimum(chunk + 1, chunks - 1)
                here = plain[which, chunk]
                joined = jnp.where(
                    low_half, pltpu.roll(here, TILE, 1), pltpu.roll(plain[which, after], TILE, 1)
                )
                pieces.append(jnp.where(jnp.broadcast_to(odd == 1, here.shape), joined, here))
        pieces.append(hh[...].astype(F32))
        return jnp.concatenate(pieces, axis=1).astype(BF16)

    def peer_at(step):
        turn, place = lax.rem(step, LAYERS), step // LAYERS
        near = jnp.where(turn == 0, 0, jnp.where(turn == LAYERS - 1, 1, turn + 1))
        place = lax.rem(place + jnp.where(near == 1, column + 1, 0), width)
        end_turn, end_place = lax.rem(step, 2), step // 2
        end_near = 1 - end_turn
        end_place = lax.rem(end_place + jnp.where(end_near == 0, column + 1, 0), width)
        near = jnp.where(at_end, end_near, near)
        place = jnp.where(at_end, end_place, place)
        return jnp.where(flip == 1, LAYERS - 1 - near, near) * width + place

    def block_copy(peer):
        return pltpu.make_async_remote_copy(
            src_ref=send.at[peer],
            dst_ref=recv.at[me],
            send_sem=send_sems.at[peer],
            recv_sem=recv_sems.at[me],
            device_id=(peer, my_sum),
            device_id_type=MESH,
        )

    def send_step(step, carry):
        peer = peer_at(step)
        send[peer] = pack(0, peer, hh_ref)
        wait_ready(peer)
        block_copy(peer).start()

        @pl.when(at_end & (flip == 0) & (step == SHARD_STEP))
        def _():
            wait_ready(partner)
            for copy in shard_copies():
                copy.start()

        return carry

    directs = jnp.where(at_end, n_pair // 2 - 1, n_pair - 1)
    lax.fori_loop(0, directs, send_step, 0)
    recv[me] = pack(0, me, hh_ref)

    spread_rows = need * 16
    spread_cols = 16 * group
    row_at = iota((spread_rows, spread_cols), 0)
    col_at = iota((spread_rows, spread_cols), 1)
    pattern[...] = jnp.where((row_at & 15) == col_at // group, row_at >> 4, -1).astype(F32)
    pair_low = iota((spread_rows, LANES), 1) < TILE
    for fetch in fetches[4:]:
        fetch.wait()
    live = iota(info_ref.shape, 0) < count_ref[...]
    positions = jnp.where(live, info_ref[...], -2).astype(F32).astype(BF16)
    repeat = jnp.where(
        iota((group, spread_cols), 0) == lax.rem(iota((group, spread_cols), 1), group), 1.0, 0.0
    ).astype(BF16)
    pos_ref[...] = lax.dot_general(
        positions, repeat, (((0,), (0,)), ((), ())), preferred_element_type=F32
    )

    def spread(tile):
        picked = jnp.where(pattern[...] == pos_ref[pl.ds(tile, 1), :], 1.0, 0.0).astype(BF16)
        base = pl.multiple_of(tile * group, group)
        halves = []
        for half in range(2):
            stack = [
                ints[pl.ds(base, group), (half * 16 + k) * LANES : (half * 16 + k + 1) * LANES]
                for k in range(16)
            ]
            halves.append(jnp.concatenate(stack, axis=0))
        stacked = jnp.concatenate(halves, axis=1)
        return jnp.dot(picked, stacked, preferred_element_type=F32)

    def spread_quad(at, carry):
        dest = at // quads
        quad = lax.rem(at, quads)
        first = dest * home_tiles + quad * 4
        for pair in range(2):
            lone = quads == 1 and 2 * pair + 1 >= home_tiles
            a = spread(first + 2 * pair)
            b = None if lone else spread(first + 2 * pair + 1)
            for half in range(2):
                a_half = a[:, half * LANES : (half + 1) * LANES]
                b_half = jnp.zeros_like(a_half) if lone else b[:, half * LANES : (half + 1) * LANES]
                even = jnp.where(pair_low, a_half, pltpu.roll(b_half, TILE, 1)).astype(BF16)
                odd = jnp.where(pair_low, pltpu.roll(a_half, TILE, 1), b_half).astype(BF16)
                cols = slice(pair * LANES, (pair + 1) * LANES)
                weights[dest, quad, :, 2 * half, :, cols] = even.reshape(need, 16, LANES)
                weights[dest, quad, :, 2 * half + 1, :, cols] = odd.reshape(need, 16, LANES)
        return carry

    lax.fori_loop(0, n_sum * quads, spread_quad, 0)

    def relay_copy(peer):
        slot = lax.rem(peer, n_pair // 2)
        return pltpu.make_async_remote_copy(
            src_ref=relay.at[slot],
            dst_ref=recv.at[partner],
            send_sem=relay_sems.at[slot],
            recv_sem=recv_sems.at[partner],
            device_id=(peer, my_sum),
            device_id_type=MESH,
        )

    def relay_peer(step):
        step = step + jnp.where(flip == 0, 0, width)
        other = lax.rem(step, n_pair // 2)
        return flip * (n_pair // 2) + other

    @pl.when(jnp.logical_not(at_end))
    def _():
        for copy in shard_copies():
            copy.wait_recv()
        unfold(1, shard_ref)

        def relay_step(step, carry):
            peer = relay_peer(step)
            block = pack(1, peer, shard_hh)

            @pl.when(peer == me)
            def _():
                recv[partner] = block

            @pl.when(peer != me)
            def _():
                relay[lax.rem(peer, n_pair // 2)] = block
                relay_copy(peer).start()

            return carry

        lax.fori_loop(0, n_pair // 2, relay_step, 0)

    occ_at = iota((slab, occ_ref.shape[1]), 1).astype(F32)
    occ_row = occ_ref[...]
    orbitals = jnp.concatenate([slab_ref[...].astype(F32), jnp.zeros((6, slab), F32)], axis=0).T
    occ_i = jnp.sum(jnp.where(orbitals[:, 0:1] == occ_at, occ_row, 0.0), axis=1, keepdims=True)
    occ_j = jnp.sum(jnp.where(orbitals[:, 1:2] == occ_at, occ_row, 0.0), axis=1, keepdims=True)
    occ_pair = occ_i + occ_j

    virt_count = virt_ref.shape[0] * LANES
    start = me * home_cols
    first_at = my_sum * (chunks * LANES // virt_count) + start // virt_count
    lane = iota((1, LANES), 1)
    first_virt = jnp.sum(
        jnp.where(lane == lax.rem(first_at, LANES), virt_ref[pl.ds(first_at // LANES, 1), :], 0.0),
        axis=1,
        keepdims=True,
    )
    pieces = []
    for at in range(home_pad // LANES):
        row = (lax.rem(start, virt_count) + at * LANES) // LANES
        here = virt_ref[pl.ds(row, 1), :]
        if home_tiles % 2:
            after = virt_ref[pl.ds(jnp.minimum(row + 1, virt_ref.shape[0] - 1), 1), :]
            joined = jnp.where(lane < TILE, pltpu.roll(here, TILE, 1), pltpu.roll(after, TILE, 1))
            odd = lax.rem(me * home_tiles, 2)
            here = jnp.where(jnp.broadcast_to(odd == 1, here.shape), joined, here)
        pieces.append(here)
    pair_row = first_virt + jnp.concatenate(pieces, axis=1)

    def arrival(peer):
        return pltpu.make_async_remote_copy(
            src_ref=send.at[peer],
            dst_ref=recv.at[peer],
            send_sem=send_sems.at[peer],
            recv_sem=recv_sems.at[peer],
            device_id=(peer, my_sum),
            device_id_type=MESH,
        )

    def take_step(step, carry):
        for side in range(2):
            peer = 2 * step + side

            mine = jnp.logical_not(at_end) & (peer == partner)

            @pl.when((peer != me) & jnp.logical_not(mine))
            def _():
                arrival(peer).wait_recv()

        both = recv[pl.ds(2 * step, 2), :, :pick_cols].astype(F32).reshape(2 * rows, pick_cols)
        left[pl.ds(pl.multiple_of(step * 2 * rows, 2 * rows), 2 * rows), :] = both.astype(BF16)
        return carry

    lax.fori_loop(0, n_pair // 2, take_step, 0)

    def part_of(dest):
        terms = []
        for quad in range(quads):
            right = weights[dest, quad].reshape(need * TILE, 256)
            terms.append(jnp.dot(left[...], right, preferred_element_type=F32))
        return jnp.concatenate(terms, axis=1).astype(BF16)

    def part_copy(dest):
        return pltpu.make_async_remote_copy(
            src_ref=part_send.at[dest],
            dst_ref=part_recv.at[my_sum],
            send_sem=part_send_sems.at[dest],
            recv_sem=part_recv_sems.at[my_sum],
            device_id=(me, dest),
            device_id_type=MESH,
        )

    def part_start(dest):
        @pl.when(dest > my_sum)
        def _():
            pl.semaphore_wait(ready_sum.at[dest], 1)

        part_copy(dest).start()

    for step in range(1, n_sum):
        dest = lax.rem(my_sum + step, n_sum)
        part_send[dest] = part_of(dest)
        if step > 1:
            part_start(lax.rem(my_sum + step - 1, n_sum))
    home = recv[:, :, pick_cols : pick_cols + home_pad].astype(F32).reshape(slab, home_pad)
    part_start(lax.rem(my_sum + n_sum - 1, n_sum))
    hh_all = recv[:, :, pick_cols + home_pad :].astype(F32).reshape(slab, slab).astype(BF16)
    total = (pair_row - occ_pair) * home + jnp.dot(
        hh_all, home.astype(BF16), preferred_element_type=F32
    )
    total = total + part_of(my_sum).astype(F32)
    for step in range(1, n_sum):
        dest = lax.rem(my_sum + step, n_sum)
        pltpu.make_async_remote_copy(
            src_ref=part_send.at[dest],
            dst_ref=part_recv.at[dest],
            send_sem=part_send_sems.at[dest],
            recv_sem=part_recv_sems.at[dest],
            device_id=(me, dest),
            device_id_type=MESH,
        ).wait()
        total = total + part_recv[dest].astype(F32)
    out_ref[...] = total[:, :home_cols]

    def sent_step(step, carry):
        block_copy(peer_at(step)).wait_send()
        return carry

    lax.fori_loop(0, directs, sent_step, 0)

    def relayed_step(step, carry):
        peer = relay_peer(step)

        @pl.when(peer != me)
        def _():
            relay_copy(peer).wait_send()

        return carry

    @pl.when(jnp.logical_not(at_end))
    def _():
        lax.fori_loop(0, n_pair // 2, relayed_step, 0)

    @pl.when(at_end)
    def _():
        for copy in shard_copies():
            copy.wait_send()


def body(
    amps,
    amp_mask,
    hh_ints,
    integrals,
    slot_info,
    slot_count,
    need_tiles,
    slab_pairs,
    occ_energy,
    virt_energy,
):
    n_pair = lax.axis_size("pair")
    n_sum = lax.axis_size("sum")
    rows = amps.shape[0]
    cols = amps.shape[2]
    chunks = cols // LANES
    home_cols = cols // n_pair
    home_tiles = home_cols // TILE
    need = need_tiles.shape[2]
    owned, group = slot_info.shape[2], slot_info.shape[3]
    slab = rows * n_pair
    virt = virt_energy.shape[0]
    assert home_cols % TILE == 0 and virt % home_cols == 0 and cols % LANES == 0
    assert home_tiles % 4 == 0 or home_tiles < 4
    quads = -(-home_tiles // 4)
    home_pad = quads * 256
    block_cols = need * TILE + home_pad + slab

    vmem = pl.BlockSpec(memory_space=pltpu.VMEM)
    anywhere = pl.BlockSpec(memory_space=pltpu.HBM)
    dims = (n_pair, n_sum, rows, chunks, need, group, home_tiles, quads)
    residual = pl.pallas_call(
        functools.partial(ladder_kernel, dims),
        out_shape=pltpu.VMEM((slab, home_cols), F32),
        in_specs=[anywhere] * 10,
        out_specs=vmem,
        scratch_shapes=[
            pltpu.SMEM(amp_mask.shape, I32),
            pltpu.SMEM((n_pair, need), I32),
            pltpu.VMEM((rows, cols), BF16),
            pltpu.VMEM(hh_ints.shape, BF16),
            pltpu.VMEM((group, owned), I32),
            pltpu.VMEM((1, owned), I32),
            pltpu.VMEM((2, slab), I32),
            pltpu.VMEM((1, occ_energy.shape[0]), F32),
            pltpu.VMEM((virt // LANES, LANES), F32),
            pltpu.VMEM((owned, 16 * group), F32),
            pltpu.VMEM((2, chunks, rows, LANES), F32),
            pltpu.VMEM((2, 2 * chunks, rows, LANES), F32),
            pltpu.VMEM((2, 2 * chunks, rows, LANES), F32),
            pltpu.VMEM((need * 16, 16 * group), F32),
            pltpu.VMEM((owned * group, TILE * TILE), BF16),
            pltpu.VMEM((n_sum, quads, need, 4, 16, 256), BF16),
            pltpu.VMEM((n_pair, rows, block_cols), BF16),
            pltpu.VMEM((n_pair, rows, block_cols), BF16),
            pltpu.VMEM((slab, need * TILE), BF16),
            pltpu.VMEM((n_sum, slab, home_pad), BF16),
            pltpu.VMEM((n_sum, slab, home_pad), BF16),
            pltpu.VMEM((rows, cols), BF16),
            pltpu.VMEM((rows, slab), BF16),
            pltpu.VMEM((n_pair // 2, rows, block_cols), BF16),
            pltpu.SemaphoreType.REGULAR((n_pair,)),
            pltpu.SemaphoreType.REGULAR((n_sum,)),
            pltpu.SemaphoreType.DMA((10,)),
            pltpu.SemaphoreType.DMA((n_pair,)),
            pltpu.SemaphoreType.DMA((n_pair,)),
            pltpu.SemaphoreType.DMA((n_sum,)),
            pltpu.SemaphoreType.DMA((n_sum,)),
            pltpu.SemaphoreType.DMA((2,)),
            pltpu.SemaphoreType.DMA((2,)),
            pltpu.SemaphoreType.DMA((n_pair // 2,)),
        ],
        compiler_params=pltpu.CompilerParams(
            collective_id=0, has_side_effects=True, vmem_limit_bytes=56 * 1024 * 1024
        ),
    )(
        amp_mask,
        need_tiles.reshape(n_pair, need),
        amps.reshape(rows, cols),
        hh_ints,
        slot_info.reshape(owned, group).T,
        slot_count.reshape(1, owned),
        slab_pairs.T,
        occ_energy.reshape(1, -1),
        virt_energy.reshape(virt // LANES, LANES),
        integrals.reshape(owned * group, TILE * TILE),
    )
    return residual.reshape(slab, 1, home_cols)


def solution(mesh):
    return jax.shard_map(
        body,
        mesh=mesh,
        in_specs=(
            P("pair", "sum", None),
            P("sum", None),
            P("pair", None),
            P("pair", "sum", None, None),
            P("pair", "sum", None, None),
            P("pair", "sum", None),
            P(None, "sum", None),
            P(),
            P(),
            P(),
        ),
        out_specs=P(None, "sum", "pair"),
        check_vma=False,
    )
```

```python
import functools

import jax
import jax.numpy as jnp
from jax import lax
from jax.experimental import pallas as pl
from jax.experimental.pallas import tpu as pltpu
from jax.sharding import PartitionSpec as P

TILE = 64
LANES = 128
LAYERS = 4
EARLY = 2
MESH = pl.DeviceIdType.MESH
BF16 = jnp.bfloat16
F32 = jnp.float32
I32 = jnp.int32


def iota(shape, axis):
    return lax.broadcasted_iota(I32, shape, axis)


def ladder_kernel(
    dims,
    mask_in,
    need_in,
    amps_in,
    hh_in,
    info_in,
    count_in,
    slab_in,
    occ_in,
    virt_in,
    ints_in,
    out_ref,
    mask_ref,
    need_ref,
    amps_ref,
    hh_ref,
    info_ref,
    count_ref,
    slab_ref,
    occ_ref,
    virt_ref,
    pos_ref,
    plain,
    low,
    high,
    pattern,
    ints,
    weights,
    send,
    recv,
    left,
    part_send,
    part_recv,
    shard_ref,
    shard_hh,
    relay,
    ready,
    ready_sum,
    in_sems,
    send_sems,
    recv_sems,
    part_send_sems,
    part_recv_sems,
    shard_send_sems,
    shard_recv_sems,
    relay_sems,
):
    n_pair, n_sum, rows, chunks, need, group, home_tiles, quads = dims
    slab = rows * n_pair
    home_pad = quads * 256
    home_cols = home_tiles * TILE
    pick_cols = need * TILE
    me = lax.axis_index("pair")
    my_sum = lax.axis_index("sum")

    width = n_pair // LAYERS
    layer, column = me // width, lax.rem(me, width)
    flip = layer // 2
    at_end = layer == flip * (LAYERS - 1)
    partner = lax.rem(me + n_pair // 2, n_pair)

    barrier = pltpu.get_barrier_semaphore()

    def greet(peer, carry):
        pl.semaphore_signal(barrier, inc=1, device_id=(peer, my_sum), device_id_type=MESH)
        return carry

    def greet_sum(peer, carry):
        pl.semaphore_signal(barrier, inc=1, device_id=(me, peer), device_id_type=MESH)
        return carry

    pairs_of_refs = (
        (mask_in, mask_ref),
        (amps_in, amps_ref),
        (need_in, need_ref),
        (hh_in, hh_ref),
        (info_in, info_ref),
        (count_in, count_ref),
        (slab_in, slab_ref),
        (occ_in, occ_ref),
        (virt_in, virt_ref),
        (ints_in, ints),
    )
    fetches = [
        pltpu.make_async_copy(src, dst, in_sems.at[at]) for at, (src, dst) in enumerate(pairs_of_refs)
    ]
    for fetch in fetches:
        fetch.start()
    lax.fori_loop(me + 1, n_pair, greet, 0)
    lax.fori_loop(my_sum + 1, n_sum, greet_sum, 0)

    @pl.when(me + my_sum > 0)
    def _():
        pl.semaphore_wait(barrier, me + my_sum)

    def answer(peer, carry):
        @pl.when((peer >= width) | (flip == 0) | (peer == partner))
        def _():
            pl.semaphore_signal(
                ready.at[me], inc=1, device_id=(peer, my_sum), device_id_type=MESH
            )

        return carry

    def answer_sum(peer, carry):
        pl.semaphore_signal(
            ready_sum.at[my_sum], inc=1, device_id=(me, peer), device_id_type=MESH
        )
        return carry

    lax.fori_loop(0, me, answer, 0)
    lax.fori_loop(0, my_sum, answer_sum, 0)

    def wait_ready(peer):
        @pl.when(peer > me)
        def _():
            pl.semaphore_wait(ready.at[peer], 1)

    def shard_copies():
        return [
            pltpu.make_async_remote_copy(
                src_ref=src,
                dst_ref=dst,
                send_sem=shard_send_sems.at[at],
                recv_sem=shard_recv_sems.at[at],
                device_id=(partner, my_sum),
                device_id_type=MESH,
            )
            for at, (src, dst) in enumerate(((amps_in, shard_ref), (hh_in, shard_hh)))
        ]

    @pl.when(at_end & (flip == 1))
    def _():
        for copy in shard_copies():
            copy.start()

    fetches[0].wait()
    fetches[1].wait()

    low_half = iota((rows, LANES), 1) < TILE
    row_at = iota((LANES, LANES), 0)
    col_at = iota((LANES, LANES), 1)
    origin = (
        (col_at & 64) + (col_at & 32) + ((col_at & 15) << 1) + ((col_at >> 4) & 1)
    )
    shuffle = jnp.where(row_at == origin, 1.0, 0.0).astype(BF16)

    def unfold(which, source):
        for chunk in range(chunks):
            keep = jnp.where(low_half, mask_ref[0, 2 * chunk], mask_ref[0, 2 * chunk + 1]).astype(F32)
            values = source[:, chunk * LANES : (chunk + 1) * LANES].astype(F32)
            plain[which, chunk] = values * keep
        moved = jnp.dot(
            plain[which].reshape(chunks * rows, LANES).astype(BF16),
            shuffle,
            preferred_element_type=F32,
        )
        turned = pltpu.roll(moved, TILE, 1)
        moved = moved.reshape(chunks, rows, LANES)
        turned = turned.reshape(chunks, rows, LANES)
        low[which] = jnp.stack([moved, turned], axis=1).reshape(2 * chunks, rows, LANES)
        high[which] = jnp.stack([turned, moved], axis=1).reshape(2 * chunks, rows, LANES)

    unfold(0, amps_ref)

    fetches[2].wait()
    fetches[3].wait()

    def pack(which, peer, hh):
        pieces = []
        for at in range(need // 2):
            first = need_ref[peer, 2 * at]
            second = need_ref[peer, 2 * at + 1]
            pieces.append(jnp.where(low_half, low[which, first], high[which, second]))
        for at in range(home_pad // LANES):
            if home_tiles % 2 == 0:
                pieces.append(plain[which, peer * (home_tiles // 2) + at])
            else:
                first = peer * home_tiles + 2 * at
                odd = lax.rem(first, 2)
                chunk = first // 2
                after = jnp.minimum(chunk + 1, chunks - 1)
                here = plain[which, chunk]
                joined = jnp.where(
                    low_half, pltpu.roll(here, TILE, 1), pltpu.roll(plain[which, after], TILE, 1)
                )
                pieces.append(jnp.where(jnp.broadcast_to(odd == 1, here.shape), joined, here))
        pieces.append(hh[...].astype(F32))
        return jnp.concatenate(pieces, axis=1).astype(BF16)

    def place(to_layer, turn):
        ahead = jnp.where(turn == 0, 0, 1 + lax.rem(column + turn, width - 1))
        beside = lax.rem(column + turn + jnp.where(to_layer == layer, 1, 0), width)
        return to_layer * width + jnp.where(to_layer == 0, ahead, beside)

    def peer_at(step):
        own = width - 1
        low_step, high_step = step - width - own, step - 2 * width
        low_layer = jnp.where(step < width, 0, jnp.where(low_step < 0, 1, 2 + lax.rem(low_step, 2)))
        low_turn = jnp.where(step < width, step, jnp.where(low_step < 0, step - width, low_step // 2))
        high_layer = jnp.where(high_step < 0, lax.rem(step, 2), jnp.where(high_step < own, 2, 3))
        high_turn = jnp.where(
            high_step < 0, step // 2, jnp.where(high_step < own, high_step, high_step - own)
        )
        end_layer = jnp.where(step < own, layer, 1 + flip)
        end_turn = jnp.where(step < own, step, step - own)
        to_layer = jnp.where(at_end, end_layer, jnp.where(flip == 0, low_layer, high_layer))
        turn = jnp.where(at_end, end_turn, jnp.where(flip == 0, low_turn, high_turn))
        own_place = layer * width + lax.rem(column + turn + 1, width)
        return jnp.where(to_layer == layer, own_place, place(to_layer, turn))

    def block_copy(peer):
        return pltpu.make_async_remote_copy(
            src_ref=send.at[peer],
            dst_ref=recv.at[me],
            send_sem=send_sems.at[peer],
            recv_sem=recv_sems.at[me],
            device_id=(peer, my_sum),
            device_id_type=MESH,
        )

    def send_step(step, carry):
        peer = peer_at(step)
        send[peer] = pack(0, peer, hh_ref)
        wait_ready(peer)
        block_copy(peer).start()

        @pl.when(at_end & (flip == 0) & (step == width - 2 + EARLY))
        def _():
            wait_ready(partner)
            for copy in shard_copies():
                copy.start()

        return carry

    directs = jnp.where(at_end, n_pair // 2 - 1, n_pair - 1)
    lax.fori_loop(0, directs, send_step, 0)
    recv[me] = pack(0, me, hh_ref)

    spread_rows = need * 16
    spread_cols = 16 * group
    row_at = iota((spread_rows, spread_cols), 0)
    col_at = iota((spread_rows, spread_cols), 1)
    pattern[...] = jnp.where((row_at & 15) == col_at // group, row_at >> 4, -1).astype(F32)
    pair_low = iota((spread_rows, LANES), 1) < TILE
    for fetch in fetches[4:]:
        fetch.wait()
    live = iota(info_ref.shape, 0) < count_ref[...]
    positions = jnp.where(live, info_ref[...], -2).astype(F32).astype(BF16)
    repeat = jnp.where(
        iota((group, spread_cols), 0) == lax.rem(iota((group, spread_cols), 1), group), 1.0, 0.0
    ).astype(BF16)
    pos_ref[...] = lax.dot_general(
        positions, repeat, (((0,), (0,)), ((), ())), preferred_element_type=F32
    )

    def spread(tile):
        picked = jnp.where(pattern[...] == pos_ref[pl.ds(tile, 1), :], 1.0, 0.0).astype(BF16)
        base = pl.multiple_of(tile * group, group)
        halves = []
        for half in range(2):
            stack = [
                ints[pl.ds(base, group), (half * 16 + k) * LANES : (half * 16 + k + 1) * LANES]
                for k in range(16)
            ]
            halves.append(jnp.concatenate(stack, axis=0))
        stacked = jnp.concatenate(halves, axis=1)
        return jnp.dot(picked, stacked, preferred_element_type=F32)

    def spread_quad(at, carry):
        dest = at // quads
        quad = lax.rem(at, quads)
        first = dest * home_tiles + quad * 4
        for pair in range(2):
            lone = quads == 1 and 2 * pair + 1 >= home_tiles
            a = spread(first + 2 * pair)
            b = None if lone else spread(first + 2 * pair + 1)
            for half in range(2):
                a_half = a[:, half * LANES : (half + 1) * LANES]
                b_half = jnp.zeros_like(a_half) if lone else b[:, half * LANES : (half + 1) * LANES]
                even = jnp.where(pair_low, a_half, pltpu.roll(b_half, TILE, 1)).astype(BF16)
                odd = jnp.where(pair_low, pltpu.roll(a_half, TILE, 1), b_half).astype(BF16)
                cols = slice(pair * LANES, (pair + 1) * LANES)
                weights[dest, quad, :, 2 * half, :, cols] = even.reshape(need, 16, LANES)
                weights[dest, quad, :, 2 * half + 1, :, cols] = odd.reshape(need, 16, LANES)
        return carry

    lax.fori_loop(0, n_sum * quads, spread_quad, 0)

    def relay_copy(peer):
        slot = lax.rem(peer, n_pair // 2)
        return pltpu.make_async_remote_copy(
            src_ref=relay.at[slot],
            dst_ref=recv.at[partner],
            send_sem=relay_sems.at[slot],
            recv_sem=recv_sems.at[partner],
            device_id=(peer, my_sum),
            device_id_type=MESH,
        )

    def relay_peer(step):
        near = jnp.where(flip == 0, step // width, 1 - step // width)
        return place(flip * 2 + near, lax.rem(step, width))

    @pl.when(jnp.logical_not(at_end))
    def _():
        for copy in shard_copies():
            copy.wait_recv()
        unfold(1, shard_ref)

        def relay_step(step, carry):
            peer = relay_peer(step)
            block = pack(1, peer, shard_hh)

            @pl.when(peer == me)
            def _():
                recv[partner] = block

            @pl.when(peer != me)
            def _():
                relay[lax.rem(peer, n_pair // 2)] = block
                relay_copy(peer).start()

            return carry

        lax.fori_loop(0, n_pair // 2, relay_step, 0)

    occ_at = iota((slab, occ_ref.shape[1]), 1).astype(F32)
    occ_row = occ_ref[...]
    orbitals = jnp.concatenate([slab_ref[...].astype(F32), jnp.zeros((6, slab), F32)], axis=0).T
    occ_i = jnp.sum(jnp.where(orbitals[:, 0:1] == occ_at, occ_row, 0.0), axis=1, keepdims=True)
    occ_j = jnp.sum(jnp.where(orbitals[:, 1:2] == occ_at, occ_row, 0.0), axis=1, keepdims=True)
    occ_pair = occ_i + occ_j

    virt_count = virt_ref.shape[0] * LANES
    start = me * home_cols
    first_at = my_sum * (chunks * LANES // virt_count) + start // virt_count
    lane = iota((1, LANES), 1)
    first_virt = jnp.sum(
        jnp.where(lane == lax.rem(first_at, LANES), virt_ref[pl.ds(first_at // LANES, 1), :], 0.0),
        axis=1,
        keepdims=True,
    )
    pieces = []
    for at in range(home_pad // LANES):
        row = (lax.rem(start, virt_count) + at * LANES) // LANES
        here = virt_ref[pl.ds(row, 1), :]
        if home_tiles % 2:
            after = virt_ref[pl.ds(jnp.minimum(row + 1, virt_ref.shape[0] - 1), 1), :]
            joined = jnp.where(lane < TILE, pltpu.roll(here, TILE, 1), pltpu.roll(after, TILE, 1))
            odd = lax.rem(me * home_tiles, 2)
            here = jnp.where(jnp.broadcast_to(odd == 1, here.shape), joined, here)
        pieces.append(here)
    pair_row = first_virt + jnp.concatenate(pieces, axis=1)

    def arrival(peer):
        return pltpu.make_async_remote_copy(
            src_ref=send.at[peer],
            dst_ref=recv.at[peer],
            send_sem=send_sems.at[peer],
            recv_sem=recv_sems.at[peer],
            device_id=(peer, my_sum),
            device_id_type=MESH,
        )

    def take_step(step, carry):
        for side in range(2):
            peer = 2 * step + side

            mine = jnp.logical_not(at_end) & (peer == partner)

            @pl.when((peer != me) & jnp.logical_not(mine))
            def _():
                arrival(peer).wait_recv()

        both = recv[pl.ds(2 * step, 2), :, :pick_cols].astype(F32).reshape(2 * rows, pick_cols)
        left[pl.ds(pl.multiple_of(step * 2 * rows, 2 * rows), 2 * rows), :] = both.astype(BF16)
        return carry

    lax.fori_loop(0, n_pair // 2, take_step, 0)

    def part_of(dest):
        terms = []
        for quad in range(quads):
            right = weights[dest, quad].reshape(need * TILE, 256)
            terms.append(jnp.dot(left[...], right, preferred_element_type=F32))
        return jnp.concatenate(terms, axis=1).astype(BF16)

    def part_copy(dest):
        return pltpu.make_async_remote_copy(
            src_ref=part_send.at[dest],
            dst_ref=part_recv.at[my_sum],
            send_sem=part_send_sems.at[dest],
            recv_sem=part_recv_sems.at[my_sum],
            device_id=(me, dest),
            device_id_type=MESH,
        )

    def part_start(dest):
        @pl.when(dest > my_sum)
        def _():
            pl.semaphore_wait(ready_sum.at[dest], 1)

        part_copy(dest).start()

    for step in range(1, n_sum):
        dest = lax.rem(my_sum + step, n_sum)
        part_send[dest] = part_of(dest)
        if step > 1:
            part_start(lax.rem(my_sum + step - 1, n_sum))
    home = recv[:, :, pick_cols : pick_cols + home_pad].astype(F32).reshape(slab, home_pad)
    part_start(lax.rem(my_sum + n_sum - 1, n_sum))
    hh_all = recv[:, :, pick_cols + home_pad :].astype(F32).reshape(slab, slab).astype(BF16)
    total = (pair_row - occ_pair) * home + jnp.dot(
        hh_all, home.astype(BF16), preferred_element_type=F32
    )
    total = total + part_of(my_sum).astype(F32)
    for step in range(1, n_sum):
        dest = lax.rem(my_sum + step, n_sum)
        pltpu.make_async_remote_copy(
            src_ref=part_send.at[dest],
            dst_ref=part_recv.at[dest],
            send_sem=part_send_sems.at[dest],
            recv_sem=part_recv_sems.at[dest],
            device_id=(me, dest),
            device_id_type=MESH,
        ).wait()
        total = total + part_recv[dest].astype(F32)
    if out_ref.shape[1] == LANES:
        lines = home_cols // LANES
        for at in range(lines):
            out_ref[pl.ds(at, slab, stride=lines), :] = total[:, at * LANES : (at + 1) * LANES]
    else:
        out_ref[...] = total[:, :home_cols]

    def sent_step(step, carry):
        block_copy(peer_at(step)).wait_send()
        return carry

    lax.fori_loop(0, directs, sent_step, 0)

    def relayed_step(step, carry):
        peer = relay_peer(step)

        @pl.when(peer != me)
        def _():
            relay_copy(peer).wait_send()

        return carry

    @pl.when(jnp.logical_not(at_end))
    def _():
        lax.fori_loop(0, n_pair // 2, relayed_step, 0)

    @pl.when(at_end)
    def _():
        for copy in shard_copies():
            copy.wait_send()


def body(
    amps,
    amp_mask,
    hh_ints,
    integrals,
    slot_info,
    slot_count,
    need_tiles,
    slab_pairs,
    occ_energy,
    virt_energy,
):
    n_pair = lax.axis_size("pair")
    n_sum = lax.axis_size("sum")
    rows = amps.shape[0]
    cols = amps.shape[2]
    chunks = cols // LANES
    home_cols = cols // n_pair
    home_tiles = home_cols // TILE
    need = need_tiles.shape[2]
    owned, group = slot_info.shape[2], slot_info.shape[3]
    slab = rows * n_pair
    virt = virt_energy.shape[0]
    assert home_cols % TILE == 0 and virt % home_cols == 0 and cols % LANES == 0
    assert home_tiles % 4 == 0 or home_tiles < 4
    quads = -(-home_tiles // 4)
    home_pad = quads * 256
    block_cols = need * TILE + home_pad + slab

    out_shape = (slab, home_cols) if home_cols % LANES else (slab * home_cols // LANES, LANES)

    vmem = pl.BlockSpec(memory_space=pltpu.VMEM)
    anywhere = pl.BlockSpec(memory_space=pltpu.HBM)
    dims = (n_pair, n_sum, rows, chunks, need, group, home_tiles, quads)
    residual = pl.pallas_call(
        functools.partial(ladder_kernel, dims),
        out_shape=pltpu.VMEM(out_shape, F32),
        in_specs=[anywhere] * 10,
        out_specs=vmem,
        scratch_shapes=[
            pltpu.SMEM(amp_mask.shape, I32),
            pltpu.SMEM((n_pair, need), I32),
            pltpu.VMEM((rows, cols), BF16),
            pltpu.VMEM(hh_ints.shape, BF16),
            pltpu.VMEM((group, owned), I32),
            pltpu.VMEM((1, owned), I32),
            pltpu.VMEM((2, slab), I32),
            pltpu.VMEM((1, occ_energy.shape[0]), F32),
            pltpu.VMEM((virt // LANES, LANES), F32),
            pltpu.VMEM((owned, 16 * group), F32),
            pltpu.VMEM((2, chunks, rows, LANES), F32),
            pltpu.VMEM((2, 2 * chunks, rows, LANES), F32),
            pltpu.VMEM((2, 2 * chunks, rows, LANES), F32),
            pltpu.VMEM((need * 16, 16 * group), F32),
            pltpu.VMEM((owned * group, TILE * TILE), BF16),
            pltpu.VMEM((n_sum, quads, need, 4, 16, 256), BF16),
            pltpu.VMEM((n_pair, rows, block_cols), BF16),
            pltpu.VMEM((n_pair, rows, block_cols), BF16),
            pltpu.VMEM((slab, need * TILE), BF16),
            pltpu.VMEM((n_sum, slab, home_pad), BF16),
            pltpu.VMEM((n_sum, slab, home_pad), BF16),
            pltpu.VMEM((rows, cols), BF16),
            pltpu.VMEM((rows, slab), BF16),
            pltpu.VMEM((n_pair // 2, rows, block_cols), BF16),
            pltpu.SemaphoreType.REGULAR((n_pair,)),
            pltpu.SemaphoreType.REGULAR((n_sum,)),
            pltpu.SemaphoreType.DMA((10,)),
            pltpu.SemaphoreType.DMA((n_pair,)),
            pltpu.SemaphoreType.DMA((n_pair,)),
            pltpu.SemaphoreType.DMA((n_sum,)),
            pltpu.SemaphoreType.DMA((n_sum,)),
            pltpu.SemaphoreType.DMA((2,)),
            pltpu.SemaphoreType.DMA((2,)),
            pltpu.SemaphoreType.DMA((n_pair // 2,)),
        ],
        compiler_params=pltpu.CompilerParams(
            collective_id=0, has_side_effects=True, vmem_limit_bytes=56 * 1024 * 1024
        ),
    )(
        amp_mask,
        need_tiles.reshape(n_pair, need),
        amps.reshape(rows, cols),
        hh_ints,
        slot_info.reshape(owned, group).T,
        slot_count.reshape(1, owned),
        slab_pairs.T,
        occ_energy.reshape(1, -1),
        virt_energy.reshape(virt // LANES, LANES),
        integrals.reshape(owned * group, TILE * TILE),
    )
    return residual.reshape(slab, 1, home_cols)


def solution(mesh):
    return jax.shard_map(
        body,
        mesh=mesh,
        in_specs=(
            P("pair", "sum", None),
            P("sum", None),
            P("pair", None),
            P("pair", "sum", None, None),
            P("pair", "sum", None, None),
            P("pair", "sum", None),
            P(None, "sum", None),
            P(),
            P(),
            P(),
        ),
        out_specs=P(None, "sum", "pair"),
        check_vma=False,
    )
```

```python
import functools

import jax
import jax.numpy as jnp
from jax import lax
from jax.experimental import pallas as pl
from jax.experimental.pallas import tpu as pltpu
from jax.sharding import PartitionSpec as P

TILE = 64
LANES = 128
LAYERS = 4
EARLY = 0
MESH = pl.DeviceIdType.MESH
BF16 = jnp.bfloat16
F32 = jnp.float32
I32 = jnp.int32


def iota(shape, axis):
    return lax.broadcasted_iota(I32, shape, axis)


def ladder_kernel(
    dims,
    mask_in,
    need_in,
    amps_in,
    hh_in,
    info_in,
    count_in,
    slab_in,
    occ_in,
    virt_in,
    ints_in,
    out_ref,
    mask_ref,
    need_ref,
    amps_ref,
    hh_ref,
    info_ref,
    count_ref,
    slab_ref,
    occ_ref,
    virt_ref,
    pos_ref,
    plain,
    low,
    high,
    pattern,
    ints,
    weights,
    send,
    recv,
    left,
    part_send,
    part_recv,
    shard_ref,
    shard_hh,
    relay,
    ready,
    ready_sum,
    in_sems,
    send_sems,
    recv_sems,
    part_send_sems,
    part_recv_sems,
    shard_send_sems,
    shard_recv_sems,
    relay_sems,
):
    n_pair, n_sum, rows, chunks, need, group, home_tiles, quads = dims
    slab = rows * n_pair
    home_pad = quads * 256
    home_cols = home_tiles * TILE
    pick_cols = need * TILE
    me = lax.axis_index("pair")
    my_sum = lax.axis_index("sum")

    width = n_pair // LAYERS
    layer, column = me // width, lax.rem(me, width)
    flip = layer // 2
    at_end = layer == flip * (LAYERS - 1)
    partner = lax.rem(me + n_pair // 2, n_pair)

    barrier = pltpu.get_barrier_semaphore()

    def greet(peer, carry):
        pl.semaphore_signal(barrier, inc=1, device_id=(peer, my_sum), device_id_type=MESH)
        return carry

    def greet_sum(peer, carry):
        pl.semaphore_signal(barrier, inc=1, device_id=(me, peer), device_id_type=MESH)
        return carry

    pairs_of_refs = (
        (mask_in, mask_ref),
        (amps_in, amps_ref),
        (need_in, need_ref),
        (hh_in, hh_ref),
        (info_in, info_ref),
        (count_in, count_ref),
        (slab_in, slab_ref),
        (occ_in, occ_ref),
        (virt_in, virt_ref),
        (ints_in, ints),
    )
    fetches = [
        pltpu.make_async_copy(src, dst, in_sems.at[at]) for at, (src, dst) in enumerate(pairs_of_refs)
    ]
    for fetch in fetches:
        fetch.start()
    lax.fori_loop(me + 1, n_pair, greet, 0)
    lax.fori_loop(my_sum + 1, n_sum, greet_sum, 0)

    @pl.when(me + my_sum > 0)
    def _():
        pl.semaphore_wait(barrier, me + my_sum)

    def answer(peer, carry):
        @pl.when((peer >= width) | (flip == 0) | (peer == partner))
        def _():
            pl.semaphore_signal(
                ready.at[me], inc=1, device_id=(peer, my_sum), device_id_type=MESH
            )

        return carry

    def answer_sum(peer, carry):
        pl.semaphore_signal(
            ready_sum.at[my_sum], inc=1, device_id=(me, peer), device_id_type=MESH
        )
        return carry

    lax.fori_loop(0, me, answer, 0)
    lax.fori_loop(0, my_sum, answer_sum, 0)

    def wait_ready(peer):
        @pl.when(peer > me)
        def _():
            pl.semaphore_wait(ready.at[peer], 1)

    def shard_copies():
        return [
            pltpu.make_async_remote_copy(
                src_ref=src,
                dst_ref=dst,
                send_sem=shard_send_sems.at[at],
                recv_sem=shard_recv_sems.at[at],
                device_id=(partner, my_sum),
                device_id_type=MESH,
            )
            for at, (src, dst) in enumerate(((amps_in, shard_ref), (hh_in, shard_hh)))
        ]

    @pl.when(at_end & (flip == 1))
    def _():
        for copy in shard_copies():
            copy.start()

    fetches[0].wait()
    fetches[1].wait()

    low_half = iota((rows, LANES), 1) < TILE
    row_at = iota((LANES, LANES), 0)
    col_at = iota((LANES, LANES), 1)
    origin = (
        (col_at & 64) + (col_at & 32) + ((col_at & 15) << 1) + ((col_at >> 4) & 1)
    )
    shuffle = jnp.where(row_at == origin, 1.0, 0.0).astype(BF16)

    def unfold(which, source):
        for chunk in range(chunks):
            keep = jnp.where(low_half, mask_ref[0, 2 * chunk], mask_ref[0, 2 * chunk + 1]).astype(F32)
            values = source[:, chunk * LANES : (chunk + 1) * LANES].astype(F32)
            plain[which, chunk] = values * keep
        moved = jnp.dot(
            plain[which].reshape(chunks * rows, LANES).astype(BF16),
            shuffle,
            preferred_element_type=F32,
        )
        turned = pltpu.roll(moved, TILE, 1)
        moved = moved.reshape(chunks, rows, LANES)
        turned = turned.reshape(chunks, rows, LANES)
        low[which] = jnp.stack([moved, turned], axis=1).reshape(2 * chunks, rows, LANES)
        high[which] = jnp.stack([turned, moved], axis=1).reshape(2 * chunks, rows, LANES)

    unfold(0, amps_ref)

    fetches[2].wait()
    fetches[3].wait()

    def pack(which, peer, hh):
        pieces = []
        for at in range(need // 2):
            first = need_ref[peer, 2 * at]
            second = need_ref[peer, 2 * at + 1]
            pieces.append(jnp.where(low_half, low[which, first], high[which, second]))
        for at in range(home_pad // LANES):
            if home_tiles % 2 == 0:
                pieces.append(plain[which, peer * (home_tiles // 2) + at])
            else:
                first = peer * home_tiles + 2 * at
                odd = lax.rem(first, 2)
                chunk = first // 2
                after = jnp.minimum(chunk + 1, chunks - 1)
                here = plain[which, chunk]
                joined = jnp.where(
                    low_half, pltpu.roll(here, TILE, 1), pltpu.roll(plain[which, after], TILE, 1)
                )
                pieces.append(jnp.where(jnp.broadcast_to(odd == 1, here.shape), joined, here))
        pieces.append(hh[...].astype(F32))
        return jnp.concatenate(pieces, axis=1).astype(BF16)

    def place(to_layer, turn):
        ahead = jnp.where(turn == 0, 0, 1 + lax.rem(column + turn, width - 1))
        beside = lax.rem(column + turn + jnp.where(to_layer == layer, 1, 0), width)
        return to_layer * width + jnp.where(to_layer == 0, ahead, beside)

    def peer_at(step):
        own = width - 1
        low_step, high_step = step - width - own, step - 2 * width
        low_layer = jnp.where(step < width, 0, jnp.where(low_step < 0, 1, 2 + lax.rem(low_step, 2)))
        low_turn = jnp.where(step < width, step, jnp.where(low_step < 0, step - width, low_step // 2))
        high_layer = jnp.where(high_step < 0, step // width, jnp.where(high_step < own, 2, 3))
        high_turn = jnp.where(
            high_step < 0, lax.rem(step, width), jnp.where(high_step < own, high_step, high_step - own)
        )
        end_layer = jnp.where(step < own, layer, 1 + flip)
        end_turn = jnp.where(step < own, step, step - own)
        to_layer = jnp.where(at_end, end_layer, jnp.where(flip == 0, low_layer, high_layer))
        turn = jnp.where(at_end, end_turn, jnp.where(flip == 0, low_turn, high_turn))
        own_place = layer * width + lax.rem(column + turn + 1, width)
        return jnp.where(to_layer == layer, own_place, place(to_layer, turn))

    def block_copy(peer):
        return pltpu.make_async_remote_copy(
            src_ref=send.at[peer],
            dst_ref=recv.at[me],
            send_sem=send_sems.at[peer],
            recv_sem=recv_sems.at[me],
            device_id=(peer, my_sum),
            device_id_type=MESH,
        )

    def send_step(step, carry):
        peer = peer_at(step)
        send[peer] = pack(0, peer, hh_ref)
        wait_ready(peer)
        block_copy(peer).start()

        @pl.when(at_end & (flip == 0) & (step == width - 2 + EARLY))
        def _():
            wait_ready(partner)
            for copy in shard_copies():
                copy.start()

        return carry

    directs = jnp.where(at_end, n_pair // 2 - 1, n_pair - 1)
    lax.fori_loop(0, directs, send_step, 0)
    recv[me] = pack(0, me, hh_ref)

    spread_rows = need * 16
    spread_cols = 16 * group
    row_at = iota((spread_rows, spread_cols), 0)
    col_at = iota((spread_rows, spread_cols), 1)
    pattern[...] = jnp.where((row_at & 15) == col_at // group, row_at >> 4, -1).astype(F32)
    pair_low = iota((spread_rows, LANES), 1) < TILE
    for fetch in fetches[4:]:
        fetch.wait()
    live = iota(info_ref.shape, 0) < count_ref[...]
    positions = jnp.where(live, info_ref[...], -2).astype(F32).astype(BF16)
    repeat = jnp.where(
        iota((group, spread_cols), 0) == lax.rem(iota((group, spread_cols), 1), group), 1.0, 0.0
    ).astype(BF16)
    pos_ref[...] = lax.dot_general(
        positions, repeat, (((0,), (0,)), ((), ())), preferred_element_type=F32
    )

    def spread(tile):
        picked = jnp.where(pattern[...] == pos_ref[pl.ds(tile, 1), :], 1.0, 0.0).astype(BF16)
        base = pl.multiple_of(tile * group, group)
        halves = []
        for half in range(2):
            stack = [
                ints[pl.ds(base, group), (half * 16 + k) * LANES : (half * 16 + k + 1) * LANES]
                for k in range(16)
            ]
            halves.append(jnp.concatenate(stack, axis=0))
        stacked = jnp.concatenate(halves, axis=1)
        return jnp.dot(picked, stacked, preferred_element_type=F32)

    def spread_quad(at, carry):
        dest = at // quads
        quad = lax.rem(at, quads)
        first = dest * home_tiles + quad * 4
        for pair in range(2):
            lone = quads == 1 and 2 * pair + 1 >= home_tiles
            a = spread(first + 2 * pair)
            b = None if lone else spread(first + 2 * pair + 1)
            for half in range(2):
                a_half = a[:, half * LANES : (half + 1) * LANES]
                b_half = jnp.zeros_like(a_half) if lone else b[:, half * LANES : (half + 1) * LANES]
                even = jnp.where(pair_low, a_half, pltpu.roll(b_half, TILE, 1)).astype(BF16)
                odd = jnp.where(pair_low, pltpu.roll(a_half, TILE, 1), b_half).astype(BF16)
                cols = slice(pair * LANES, (pair + 1) * LANES)
                weights[dest, quad, :, 2 * half, :, cols] = even.reshape(need, 16, LANES)
                weights[dest, quad, :, 2 * half + 1, :, cols] = odd.reshape(need, 16, LANES)
        return carry

    lax.fori_loop(0, n_sum * quads, spread_quad, 0)

    def relay_copy(peer):
        slot = lax.rem(peer, n_pair // 2)
        return pltpu.make_async_remote_copy(
            src_ref=relay.at[slot],
            dst_ref=recv.at[partner],
            send_sem=relay_sems.at[slot],
            recv_sem=recv_sems.at[partner],
            device_id=(peer, my_sum),
            device_id_type=MESH,
        )

    def relay_peer(step):
        near = jnp.where(flip == 0, step // width, 1 - step // width)
        return place(flip * 2 + near, lax.rem(step, width))

    @pl.when(jnp.logical_not(at_end))
    def _():
        for copy in shard_copies():
            copy.wait_recv()
        unfold(1, shard_ref)

        def relay_step(step, carry):
            peer = relay_peer(step)
            block = pack(1, peer, shard_hh)

            @pl.when(peer == me)
            def _():
                recv[partner] = block

            @pl.when(peer != me)
            def _():
                relay[lax.rem(peer, n_pair // 2)] = block
                relay_copy(peer).start()

            return carry

        lax.fori_loop(0, n_pair // 2, relay_step, 0)

    occ_at = iota((slab, occ_ref.shape[1]), 1).astype(F32)
    occ_row = occ_ref[...]
    orbitals = jnp.concatenate([slab_ref[...].astype(F32), jnp.zeros((6, slab), F32)], axis=0).T
    occ_i = jnp.sum(jnp.where(orbitals[:, 0:1] == occ_at, occ_row, 0.0), axis=1, keepdims=True)
    occ_j = jnp.sum(jnp.where(orbitals[:, 1:2] == occ_at, occ_row, 0.0), axis=1, keepdims=True)
    occ_pair = occ_i + occ_j

    virt_count = virt_ref.shape[0] * LANES
    start = me * home_cols
    first_at = my_sum * (chunks * LANES // virt_count) + start // virt_count
    lane = iota((1, LANES), 1)
    first_virt = jnp.sum(
        jnp.where(lane == lax.rem(first_at, LANES), virt_ref[pl.ds(first_at // LANES, 1), :], 0.0),
        axis=1,
        keepdims=True,
    )
    pieces = []
    for at in range(home_pad // LANES):
        row = (lax.rem(start, virt_count) + at * LANES) // LANES
        here = virt_ref[pl.ds(row, 1), :]
        if home_tiles % 2:
            after = virt_ref[pl.ds(jnp.minimum(row + 1, virt_ref.shape[0] - 1), 1), :]
            joined = jnp.where(lane < TILE, pltpu.roll(here, TILE, 1), pltpu.roll(after, TILE, 1))
            odd = lax.rem(me * home_tiles, 2)
            here = jnp.where(jnp.broadcast_to(odd == 1, here.shape), joined, here)
        pieces.append(here)
    pair_row = first_virt + jnp.concatenate(pieces, axis=1)

    def arrival(peer):
        return pltpu.make_async_remote_copy(
            src_ref=send.at[peer],
            dst_ref=recv.at[peer],
            send_sem=send_sems.at[peer],
            recv_sem=recv_sems.at[peer],
            device_id=(peer, my_sum),
            device_id_type=MESH,
        )

    def take_step(step, carry):
        for side in range(2):
            peer = 2 * step + side

            mine = jnp.logical_not(at_end) & (peer == partner)

            @pl.when((peer != me) & jnp.logical_not(mine))
            def _():
                arrival(peer).wait_recv()

        both = recv[pl.ds(2 * step, 2), :, :pick_cols].astype(F32).reshape(2 * rows, pick_cols)
        left[pl.ds(pl.multiple_of(step * 2 * rows, 2 * rows), 2 * rows), :] = both.astype(BF16)
        return carry

    lax.fori_loop(0, n_pair // 2, take_step, 0)

    def part_of(dest):
        terms = []
        for quad in range(quads):
            right = weights[dest, quad].reshape(need * TILE, 256)
            terms.append(jnp.dot(left[...], right, preferred_element_type=F32))
        return jnp.concatenate(terms, axis=1).astype(BF16)

    def part_copy(dest):
        return pltpu.make_async_remote_copy(
            src_ref=part_send.at[dest],
            dst_ref=part_recv.at[my_sum],
            send_sem=part_send_sems.at[dest],
            recv_sem=part_recv_sems.at[my_sum],
            device_id=(me, dest),
            device_id_type=MESH,
        )

    def part_start(dest):
        @pl.when(dest > my_sum)
        def _():
            pl.semaphore_wait(ready_sum.at[dest], 1)

        part_copy(dest).start()

    for step in range(1, n_sum):
        dest = lax.rem(my_sum + step, n_sum)
        part_send[dest] = part_of(dest)
        if step > 1:
            part_start(lax.rem(my_sum + step - 1, n_sum))
    home = recv[:, :, pick_cols : pick_cols + home_pad].astype(F32).reshape(slab, home_pad)
    part_start(lax.rem(my_sum + n_sum - 1, n_sum))
    hh_all = recv[:, :, pick_cols + home_pad :].astype(F32).reshape(slab, slab).astype(BF16)
    total = (pair_row - occ_pair) * home + jnp.dot(
        hh_all, home.astype(BF16), preferred_element_type=F32
    )
    total = total + part_of(my_sum).astype(F32)
    for step in range(1, n_sum):
        dest = lax.rem(my_sum + step, n_sum)
        pltpu.make_async_remote_copy(
            src_ref=part_send.at[dest],
            dst_ref=part_recv.at[dest],
            send_sem=part_send_sems.at[dest],
            recv_sem=part_recv_sems.at[dest],
            device_id=(me, dest),
            device_id_type=MESH,
        ).wait()
        total = total + part_recv[dest].astype(F32)
    if out_ref.shape[1] == LANES:
        lines = home_cols // LANES
        for at in range(lines):
            out_ref[pl.ds(at, slab, stride=lines), :] = total[:, at * LANES : (at + 1) * LANES]
    else:
        out_ref[...] = total[:, :home_cols]

    def sent_step(step, carry):
        block_copy(peer_at(step)).wait_send()
        return carry

    lax.fori_loop(0, directs, sent_step, 0)

    def relayed_step(step, carry):
        peer = relay_peer(step)

        @pl.when(peer != me)
        def _():
            relay_copy(peer).wait_send()

        return carry

    @pl.when(jnp.logical_not(at_end))
    def _():
        lax.fori_loop(0, n_pair // 2, relayed_step, 0)

    @pl.when(at_end)
    def _():
        for copy in shard_copies():
            copy.wait_send()


def body(
    amps,
    amp_mask,
    hh_ints,
    integrals,
    slot_info,
    slot_count,
    need_tiles,
    slab_pairs,
    occ_energy,
    virt_energy,
):
    n_pair = lax.axis_size("pair")
    n_sum = lax.axis_size("sum")
    rows = amps.shape[0]
    cols = amps.shape[2]
    chunks = cols // LANES
    home_cols = cols // n_pair
    home_tiles = home_cols // TILE
    need = need_tiles.shape[2]
    owned, group = slot_info.shape[2], slot_info.shape[3]
    slab = rows * n_pair
    virt = virt_energy.shape[0]
    assert home_cols % TILE == 0 and virt % home_cols == 0 and cols % LANES == 0
    assert home_tiles % 4 == 0 or home_tiles < 4
    quads = -(-home_tiles // 4)
    home_pad = quads * 256
    block_cols = need * TILE + home_pad + slab

    out_shape = (slab, home_cols) if home_cols % LANES else (slab * home_cols // LANES, LANES)

    vmem = pl.BlockSpec(memory_space=pltpu.VMEM)
    anywhere = pl.BlockSpec(memory_space=pltpu.HBM)
    dims = (n_pair, n_sum, rows, chunks, need, group, home_tiles, quads)
    residual = pl.pallas_call(
        functools.partial(ladder_kernel, dims),
        out_shape=pltpu.VMEM(out_shape, F32),
        in_specs=[anywhere] * 10,
        out_specs=vmem,
        scratch_shapes=[
            pltpu.SMEM(amp_mask.shape, I32),
            pltpu.SMEM((n_pair, need), I32),
            pltpu.VMEM((rows, cols), BF16),
            pltpu.VMEM(hh_ints.shape, BF16),
            pltpu.VMEM((group, owned), I32),
            pltpu.VMEM((1, owned), I32),
            pltpu.VMEM((2, slab), I32),
            pltpu.VMEM((1, occ_energy.shape[0]), F32),
            pltpu.VMEM((virt // LANES, LANES), F32),
            pltpu.VMEM((owned, 16 * group), F32),
            pltpu.VMEM((2, chunks, rows, LANES), F32),
            pltpu.VMEM((2, 2 * chunks, rows, LANES), F32),
            pltpu.VMEM((2, 2 * chunks, rows, LANES), F32),
            pltpu.VMEM((need * 16, 16 * group), F32),
            pltpu.VMEM((owned * group, TILE * TILE), BF16),
            pltpu.VMEM((n_sum, quads, need, 4, 16, 256), BF16),
            pltpu.VMEM((n_pair, rows, block_cols), BF16),
            pltpu.VMEM((n_pair, rows, block_cols), BF16),
            pltpu.VMEM((slab, need * TILE), BF16),
            pltpu.VMEM((n_sum, slab, home_pad), BF16),
            pltpu.VMEM((n_sum, slab, home_pad), BF16),
            pltpu.VMEM((rows, cols), BF16),
            pltpu.VMEM((rows, slab), BF16),
            pltpu.VMEM((n_pair // 2, rows, block_cols), BF16),
            pltpu.SemaphoreType.REGULAR((n_pair,)),
            pltpu.SemaphoreType.REGULAR((n_sum,)),
            pltpu.SemaphoreType.DMA((10,)),
            pltpu.SemaphoreType.DMA((n_pair,)),
            pltpu.SemaphoreType.DMA((n_pair,)),
            pltpu.SemaphoreType.DMA((n_sum,)),
            pltpu.SemaphoreType.DMA((n_sum,)),
            pltpu.SemaphoreType.DMA((2,)),
            pltpu.SemaphoreType.DMA((2,)),
            pltpu.SemaphoreType.DMA((n_pair // 2,)),
        ],
        compiler_params=pltpu.CompilerParams(
            collective_id=0, has_side_effects=True, vmem_limit_bytes=56 * 1024 * 1024
        ),
    )(
        amp_mask,
        need_tiles.reshape(n_pair, need),
        amps.reshape(rows, cols),
        hh_ints,
        slot_info.reshape(owned, group).T,
        slot_count.reshape(1, owned),
        slab_pairs.T,
        occ_energy.reshape(1, -1),
        virt_energy.reshape(virt // LANES, LANES),
        integrals.reshape(owned * group, TILE * TILE),
    )
    return residual.reshape(slab, 1, home_cols)


def solution(mesh):
    return jax.shard_map(
        body,
        mesh=mesh,
        in_specs=(
            P("pair", "sum", None),
            P("sum", None),
            P("pair", None),
            P("pair", "sum", None, None),
            P("pair", "sum", None, None),
            P("pair", "sum", None),
            P(None, "sum", None),
            P(),
            P(),
            P(),
        ),
        out_specs=P(None, "sum", "pair"),
        check_vma=False,
    )
```

```python
import functools

import jax
import jax.numpy as jnp
from jax import lax
from jax.experimental import pallas as pl
from jax.experimental.pallas import tpu as pltpu
from jax.sharding import PartitionSpec as P

TILE = 64
LANES = 128
LAYERS = 4
EARLY = 0
MESH = pl.DeviceIdType.MESH
BF16 = jnp.bfloat16
F32 = jnp.float32
I32 = jnp.int32


def iota(shape, axis):
    return lax.broadcasted_iota(I32, shape, axis)


def ladder_kernel(
    dims,
    mask_in,
    need_in,
    amps_in,
    hh_in,
    info_in,
    count_in,
    slab_in,
    occ_in,
    virt_in,
    ints_in,
    out_ref,
    mask_ref,
    need_ref,
    amps_ref,
    hh_ref,
    info_ref,
    count_ref,
    slab_ref,
    occ_ref,
    virt_ref,
    pos_ref,
    plain,
    low,
    high,
    pattern,
    ints,
    weights,
    send,
    recv,
    left,
    own_part,
    part_send,
    part_recv,
    shard_ref,
    shard_hh,
    relay,
    ready,
    ready_sum,
    in_sems,
    send_sems,
    recv_sems,
    part_send_sems,
    part_recv_sems,
    shard_send_sems,
    shard_recv_sems,
    relay_sems,
):
    n_pair, n_sum, rows, chunks, need, group, home_tiles, quads = dims
    slab = rows * n_pair
    home_pad = quads * 256
    home_cols = home_tiles * TILE
    pick_cols = need * TILE
    me = lax.axis_index("pair")
    my_sum = lax.axis_index("sum")

    width = n_pair // LAYERS
    layer, column = me // width, lax.rem(me, width)
    flip = layer // 2
    at_end = layer == flip * (LAYERS - 1)
    partner = lax.rem(me + n_pair // 2, n_pair)

    barrier = pltpu.get_barrier_semaphore()

    def greet(peer, carry):
        pl.semaphore_signal(barrier, inc=1, device_id=(peer, my_sum), device_id_type=MESH)
        return carry

    def greet_sum(peer, carry):
        pl.semaphore_signal(barrier, inc=1, device_id=(me, peer), device_id_type=MESH)
        return carry

    pairs_of_refs = (
        (mask_in, mask_ref),
        (amps_in, amps_ref),
        (need_in, need_ref),
        (hh_in, hh_ref),
        (info_in, info_ref),
        (count_in, count_ref),
        (slab_in, slab_ref),
        (occ_in, occ_ref),
        (virt_in, virt_ref),
        (ints_in, ints),
    )
    fetches = [
        pltpu.make_async_copy(src, dst, in_sems.at[at]) for at, (src, dst) in enumerate(pairs_of_refs)
    ]
    for fetch in fetches:
        fetch.start()
    lax.fori_loop(me + 1, n_pair, greet, 0)
    lax.fori_loop(my_sum + 1, n_sum, greet_sum, 0)

    @pl.when(me + my_sum > 0)
    def _():
        pl.semaphore_wait(barrier, me + my_sum)

    def shard_copies():
        return [
            pltpu.make_async_remote_copy(
                src_ref=src,
                dst_ref=dst,
                send_sem=shard_send_sems.at[at],
                recv_sem=shard_recv_sems.at[at],
                device_id=(partner, my_sum),
                device_id_type=MESH,
            )
            for at, (src, dst) in enumerate(((amps_in, shard_ref), (hh_in, shard_hh)))
        ]

    @pl.when(at_end & (flip == 1))
    def _():
        for copy in shard_copies():
            copy.start()

    def answer(peer, carry):
        @pl.when((peer >= width) | (flip == 0) | (peer == partner))
        def _():
            pl.semaphore_signal(
                ready.at[me], inc=1, device_id=(peer, my_sum), device_id_type=MESH
            )

        return carry

    def answer_sum(peer, carry):
        pl.semaphore_signal(
            ready_sum.at[my_sum], inc=1, device_id=(me, peer), device_id_type=MESH
        )
        return carry

    lax.fori_loop(0, me, answer, 0)
    lax.fori_loop(0, my_sum, answer_sum, 0)

    def wait_ready(peer):
        @pl.when(peer > me)
        def _():
            pl.semaphore_wait(ready.at[peer], 1)

    fetches[0].wait()
    fetches[1].wait()

    low_half = iota((rows, LANES), 1) < TILE
    row_at = iota((LANES, LANES), 0)
    col_at = iota((LANES, LANES), 1)
    origin = (
        (col_at & 64) + (col_at & 32) + ((col_at & 15) << 1) + ((col_at >> 4) & 1)
    )
    shuffle = jnp.where(row_at == origin, 1.0, 0.0).astype(BF16)

    def unfold(which, source):
        for chunk in range(chunks):
            keep = jnp.where(low_half, mask_ref[0, 2 * chunk], mask_ref[0, 2 * chunk + 1]).astype(F32)
            values = source[:, chunk * LANES : (chunk + 1) * LANES].astype(F32)
            plain[which, chunk] = values * keep
        moved = jnp.dot(
            plain[which].reshape(chunks * rows, LANES).astype(BF16),
            shuffle,
            preferred_element_type=F32,
        )
        turned = pltpu.roll(moved, TILE, 1)
        moved = moved.reshape(chunks, rows, LANES)
        turned = turned.reshape(chunks, rows, LANES)
        low[which] = jnp.stack([moved, turned], axis=1).reshape(2 * chunks, rows, LANES)
        high[which] = jnp.stack([turned, moved], axis=1).reshape(2 * chunks, rows, LANES)

    unfold(0, amps_ref)

    fetches[2].wait()
    fetches[3].wait()

    def pack(which, peer, hh):
        pieces = []
        for at in range(need // 2):
            first = need_ref[peer, 2 * at]
            second = need_ref[peer, 2 * at + 1]
            pieces.append(jnp.where(low_half, low[which, first], high[which, second]))
        for at in range(home_pad // LANES):
            if home_tiles % 2 == 0:
                pieces.append(plain[which, peer * (home_tiles // 2) + at])
            else:
                first = peer * home_tiles + 2 * at
                odd = lax.rem(first, 2)
                chunk = first // 2
                after = jnp.minimum(chunk + 1, chunks - 1)
                here = plain[which, chunk]
                joined = jnp.where(
                    low_half, pltpu.roll(here, TILE, 1), pltpu.roll(plain[which, after], TILE, 1)
                )
                pieces.append(jnp.where(jnp.broadcast_to(odd == 1, here.shape), joined, here))
        pieces.append(hh[...].astype(F32))
        return jnp.concatenate(pieces, axis=1).astype(BF16)

    def place(to_layer, turn):
        ahead = jnp.where(turn == 0, 0, 1 + lax.rem(column + turn, width - 1))
        beside = lax.rem(column + turn + jnp.where(to_layer == layer, 1, 0), width)
        return to_layer * width + jnp.where(to_layer == 0, ahead, beside)

    def peer_at(step):
        own = width - 1
        low_step, high_step = step - width - own, step - 2 * width
        up_layer = jnp.where((low_step >= 1) & (low_step < width + 1), 3, 2)
        up_turn = jnp.where(low_step < 1, low_step, jnp.where(up_layer == 3, low_step - 1, low_step - width))
        low_layer = jnp.where(step < width, 0, jnp.where(low_step < 0, 1, up_layer))
        low_turn = jnp.where(step < width, step, jnp.where(low_step < 0, step - width, up_turn))
        high_layer = jnp.where(high_step < 0, step // width, jnp.where(high_step < own, 2, 3))
        high_turn = jnp.where(
            high_step < 0, lax.rem(step, width), jnp.where(high_step < own, high_step, high_step - own)
        )
        end_layer = jnp.where(step < own, layer, 1 + flip)
        end_turn = jnp.where(step < own, step, step - own)
        to_layer = jnp.where(at_end, end_layer, jnp.where(flip == 0, low_layer, high_layer))
        turn = jnp.where(at_end, end_turn, jnp.where(flip == 0, low_turn, high_turn))
        own_place = layer * width + lax.rem(column + turn + 1, width)
        return jnp.where(to_layer == layer, own_place, place(to_layer, turn))

    def block_copy(peer):
        return pltpu.make_async_remote_copy(
            src_ref=send.at[peer],
            dst_ref=recv.at[me],
            send_sem=send_sems.at[peer],
            recv_sem=recv_sems.at[me],
            device_id=(peer, my_sum),
            device_id_type=MESH,
        )

    def send_step(step, carry):
        peer = peer_at(step)
        send[peer] = pack(0, peer, hh_ref)
        wait_ready(peer)
        block_copy(peer).start()

        @pl.when(at_end & (flip == 0) & (step == width - 2 + EARLY))
        def _():
            wait_ready(partner)
            for copy in shard_copies():
                copy.start()

        return carry

    directs = jnp.where(at_end, n_pair // 2 - 1, n_pair - 1)
    lax.fori_loop(0, directs, send_step, 0)
    recv[me] = pack(0, me, hh_ref)

    spread_rows = need * 16
    spread_cols = 16 * group
    row_at = iota((spread_rows, spread_cols), 0)
    col_at = iota((spread_rows, spread_cols), 1)
    pattern[...] = jnp.where((row_at & 15) == col_at // group, row_at >> 4, -1).astype(F32)
    pair_low = iota((spread_rows, LANES), 1) < TILE
    for fetch in fetches[4:]:
        fetch.wait()
    live = iota(info_ref.shape, 0) < count_ref[...]
    positions = jnp.where(live, info_ref[...], -2).astype(F32).astype(BF16)
    repeat = jnp.where(
        iota((group, spread_cols), 0) == lax.rem(iota((group, spread_cols), 1), group), 1.0, 0.0
    ).astype(BF16)
    pos_ref[...] = lax.dot_general(
        positions, repeat, (((0,), (0,)), ((), ())), preferred_element_type=F32
    )

    def spread(tile):
        picked = jnp.where(pattern[...] == pos_ref[pl.ds(tile, 1), :], 1.0, 0.0).astype(BF16)
        base = pl.multiple_of(tile * group, group)
        halves = []
        for half in range(2):
            stack = [
                ints[pl.ds(base, group), (half * 16 + k) * LANES : (half * 16 + k + 1) * LANES]
                for k in range(16)
            ]
            halves.append(jnp.concatenate(stack, axis=0))
        stacked = jnp.concatenate(halves, axis=1)
        return jnp.dot(picked, stacked, preferred_element_type=F32)

    def spread_quad(at, carry):
        dest = at // quads
        quad = lax.rem(at, quads)
        first = dest * home_tiles + quad * 4
        for pair in range(2):
            lone = quads == 1 and 2 * pair + 1 >= home_tiles
            a = spread(first + 2 * pair)
            b = None if lone else spread(first + 2 * pair + 1)
            for half in range(2):
                a_half = a[:, half * LANES : (half + 1) * LANES]
                b_half = jnp.zeros_like(a_half) if lone else b[:, half * LANES : (half + 1) * LANES]
                even = jnp.where(pair_low, a_half, pltpu.roll(b_half, TILE, 1)).astype(BF16)
                odd = jnp.where(pair_low, pltpu.roll(a_half, TILE, 1), b_half).astype(BF16)
                cols = slice(pair * LANES, (pair + 1) * LANES)
                weights[dest, quad, :, 2 * half, :, cols] = even.reshape(need, 16, LANES)
                weights[dest, quad, :, 2 * half + 1, :, cols] = odd.reshape(need, 16, LANES)
        return carry

    lax.fori_loop(0, n_sum * quads, spread_quad, 0)

    def relay_copy(peer):
        slot = lax.rem(peer, n_pair // 2)
        return pltpu.make_async_remote_copy(
            src_ref=relay.at[slot],
            dst_ref=recv.at[partner],
            send_sem=relay_sems.at[slot],
            recv_sem=recv_sems.at[partner],
            device_id=(peer, my_sum),
            device_id_type=MESH,
        )

    def relay_peer(step):
        near = jnp.where(flip == 0, step // width, 1 - step // width)
        return place(flip * 2 + near, lax.rem(step, width))

    @pl.when(jnp.logical_not(at_end))
    def _():
        for copy in shard_copies():
            copy.wait_recv()
        unfold(1, shard_ref)

        def relay_step(step, carry):
            peer = relay_peer(step)
            block = pack(1, peer, shard_hh)

            @pl.when(peer == me)
            def _():
                recv[partner] = block

            @pl.when(peer != me)
            def _():
                relay[lax.rem(peer, n_pair // 2)] = block
                relay_copy(peer).start()

            return carry

        lax.fori_loop(0, n_pair // 2, relay_step, 0)

    occ_at = iota((slab, occ_ref.shape[1]), 1).astype(F32)
    occ_row = occ_ref[...]
    orbitals = jnp.concatenate([slab_ref[...].astype(F32), jnp.zeros((6, slab), F32)], axis=0).T
    occ_i = jnp.sum(jnp.where(orbitals[:, 0:1] == occ_at, occ_row, 0.0), axis=1, keepdims=True)
    occ_j = jnp.sum(jnp.where(orbitals[:, 1:2] == occ_at, occ_row, 0.0), axis=1, keepdims=True)
    occ_pair = occ_i + occ_j

    virt_count = virt_ref.shape[0] * LANES
    start = me * home_cols
    first_at = my_sum * (chunks * LANES // virt_count) + start // virt_count
    lane = iota((1, LANES), 1)
    first_virt = jnp.sum(
        jnp.where(lane == lax.rem(first_at, LANES), virt_ref[pl.ds(first_at // LANES, 1), :], 0.0),
        axis=1,
        keepdims=True,
    )
    pieces = []
    for at in range(home_pad // LANES):
        row = (lax.rem(start, virt_count) + at * LANES) // LANES
        here = virt_ref[pl.ds(row, 1), :]
        if home_tiles % 2:
            after = virt_ref[pl.ds(jnp.minimum(row + 1, virt_ref.shape[0] - 1), 1), :]
            joined = jnp.where(lane < TILE, pltpu.roll(here, TILE, 1), pltpu.roll(after, TILE, 1))
            odd = lax.rem(me * home_tiles, 2)
            here = jnp.where(jnp.broadcast_to(odd == 1, here.shape), joined, here)
        pieces.append(here)
    pair_row = first_virt + jnp.concatenate(pieces, axis=1)

    def arrival(peer):
        return pltpu.make_async_remote_copy(
            src_ref=send.at[peer],
            dst_ref=recv.at[peer],
            send_sem=send_sems.at[peer],
            recv_sem=recv_sems.at[peer],
            device_id=(peer, my_sum),
            device_id_type=MESH,
        )

    reach = n_pair // 2
    half_rows = reach * rows
    halves = (flip, 1 - flip)

    def take_half(phase):
        def take_step(step, carry):
            first = halves[phase] * reach + 2 * step
            for side in range(2):
                peer = first + side
                mine = jnp.logical_not(at_end) & (peer == partner)

                @pl.when((peer != me) & jnp.logical_not(mine))
                def _():
                    arrival(peer).wait_recv()

            both = recv[pl.ds(first, 2), :, :pick_cols].astype(F32).reshape(2 * rows, pick_cols)
            at = pl.multiple_of(step * 2 * rows, 2 * rows)
            left[phase, pl.ds(at, 2 * rows), :] = both.astype(BF16)
            return carry

        lax.fori_loop(0, reach // 2, take_step, 0)

    def part_of(phase, dest):
        terms = []
        for quad in range(quads):
            right = weights[dest, quad].reshape(need * TILE, 256)
            terms.append(jnp.dot(left[phase], right, preferred_element_type=F32))
        return jnp.concatenate(terms, axis=1).astype(BF16)

    def part_copy(phase, source, target):
        return pltpu.make_async_remote_copy(
            src_ref=part_send.at[phase, target],
            dst_ref=part_recv.at[phase, source],
            send_sem=part_send_sems.at[phase, target],
            recv_sem=part_recv_sems.at[phase, source],
            device_id=(me, target),
            device_id_type=MESH,
        )

    def other_sums():
        return [lax.rem(my_sum + step, n_sum) for step in range(1, n_sum)]

    take_half(0)
    for dest in other_sums():
        part_send[0, dest] = part_of(0, dest)

        @pl.when(dest > my_sum)
        def _():
            pl.semaphore_wait(ready_sum.at[dest], 1)

        part_copy(0, my_sum, dest).start()
    own_part[...] = part_of(0, my_sum)

    take_half(1)
    for dest in other_sums():
        part_send[1, dest] = part_of(1, dest)
        part_copy(1, my_sum, dest).start()
    home = recv[:, :, pick_cols : pick_cols + home_pad].astype(F32).reshape(slab, home_pad)
    home = home.astype(BF16)
    totals = []
    for phase in range(2):
        own = own_part[...] if phase == 0 else part_of(1, my_sum)
        lines = pl.ds(halves[phase] * reach, reach)
        here = recv[lines, :, pick_cols : pick_cols + home_pad].astype(F32)
        hh_rows = recv[lines, :, pick_cols + home_pad :].astype(F32)
        occ_rows = jnp.where(flip == phase, occ_pair[:half_rows], occ_pair[half_rows:])
        total = (pair_row - occ_rows) * here.reshape(half_rows, home_pad)
        total = total + jnp.dot(
            hh_rows.reshape(half_rows, slab).astype(BF16), home, preferred_element_type=F32
        )
        totals.append(total + own.astype(F32))
    for phase in range(2):
        total = totals[phase]
        for dest in other_sums():
            part_copy(phase, dest, dest).wait()
            total = total + part_recv[phase, dest].astype(F32)
        if out_ref.shape[1] == LANES:
            lines = home_cols // LANES
            base = halves[phase] * (half_rows * lines)
            for at in range(lines):
                out_ref[pl.ds(base + at, half_rows, stride=lines), :] = total[
                    :, at * LANES : (at + 1) * LANES
                ]
        else:
            base = pl.multiple_of(halves[phase] * half_rows, half_rows)
            out_ref[pl.ds(base, half_rows), :] = total[:, :home_cols]

    def sent_step(step, carry):
        block_copy(peer_at(step)).wait_send()
        return carry

    lax.fori_loop(0, directs, sent_step, 0)

    def relayed_step(step, carry):
        peer = relay_peer(step)

        @pl.when(peer != me)
        def _():
            relay_copy(peer).wait_send()

        return carry

    @pl.when(jnp.logical_not(at_end))
    def _():
        lax.fori_loop(0, n_pair // 2, relayed_step, 0)

    @pl.when(at_end)
    def _():
        for copy in shard_copies():
            copy.wait_send()


def body(
    amps,
    amp_mask,
    hh_ints,
    integrals,
    slot_info,
    slot_count,
    need_tiles,
    slab_pairs,
    occ_energy,
    virt_energy,
):
    n_pair = lax.axis_size("pair")
    n_sum = lax.axis_size("sum")
    rows = amps.shape[0]
    cols = amps.shape[2]
    chunks = cols // LANES
    home_cols = cols // n_pair
    home_tiles = home_cols // TILE
    need = need_tiles.shape[2]
    owned, group = slot_info.shape[2], slot_info.shape[3]
    slab = rows * n_pair
    virt = virt_energy.shape[0]
    assert home_cols % TILE == 0 and virt % home_cols == 0 and cols % LANES == 0
    assert home_tiles % 4 == 0 or home_tiles < 4
    quads = -(-home_tiles // 4)
    home_pad = quads * 256
    block_cols = need * TILE + home_pad + slab

    out_shape = (slab, home_cols) if home_cols % LANES else (slab * home_cols // LANES, LANES)

    vmem = pl.BlockSpec(memory_space=pltpu.VMEM)
    anywhere = pl.BlockSpec(memory_space=pltpu.HBM)
    dims = (n_pair, n_sum, rows, chunks, need, group, home_tiles, quads)
    residual = pl.pallas_call(
        functools.partial(ladder_kernel, dims),
        out_shape=pltpu.VMEM(out_shape, F32),
        in_specs=[anywhere] * 10,
        out_specs=vmem,
        scratch_shapes=[
            pltpu.SMEM(amp_mask.shape, I32),
            pltpu.SMEM((n_pair, need), I32),
            pltpu.VMEM((rows, cols), BF16),
            pltpu.VMEM(hh_ints.shape, BF16),
            pltpu.VMEM((group, owned), I32),
            pltpu.VMEM((1, owned), I32),
            pltpu.VMEM((2, slab), I32),
            pltpu.VMEM((1, occ_energy.shape[0]), F32),
            pltpu.VMEM((virt // LANES, LANES), F32),
            pltpu.VMEM((owned, 16 * group), F32),
            pltpu.VMEM((2, chunks, rows, LANES), F32),
            pltpu.VMEM((2, 2 * chunks, rows, LANES), F32),
            pltpu.VMEM((2, 2 * chunks, rows, LANES), F32),
            pltpu.VMEM((need * 16, 16 * group), F32),
            pltpu.VMEM((owned * group, TILE * TILE), BF16),
            pltpu.VMEM((n_sum, quads, need, 4, 16, 256), BF16),
            pltpu.VMEM((n_pair, rows, block_cols), BF16),
            pltpu.VMEM((n_pair, rows, block_cols), BF16),
            pltpu.VMEM((2, slab // 2, need * TILE), BF16),
            pltpu.VMEM((slab // 2, home_pad), BF16),
            pltpu.VMEM((2, n_sum, slab // 2, home_pad), BF16),
            pltpu.VMEM((2, n_sum, slab // 2, home_pad), BF16),
            pltpu.VMEM((rows, cols), BF16),
            pltpu.VMEM((rows, slab), BF16),
            pltpu.VMEM((n_pair // 2, rows, block_cols), BF16),
            pltpu.SemaphoreType.REGULAR((n_pair,)),
            pltpu.SemaphoreType.REGULAR((n_sum,)),
            pltpu.SemaphoreType.DMA((10,)),
            pltpu.SemaphoreType.DMA((n_pair,)),
            pltpu.SemaphoreType.DMA((n_pair,)),
            pltpu.SemaphoreType.DMA((2, n_sum)),
            pltpu.SemaphoreType.DMA((2, n_sum)),
            pltpu.SemaphoreType.DMA((2,)),
            pltpu.SemaphoreType.DMA((2,)),
            pltpu.SemaphoreType.DMA((n_pair // 2,)),
        ],
        compiler_params=pltpu.CompilerParams(
            collective_id=0, has_side_effects=True, vmem_limit_bytes=56 * 1024 * 1024
        ),
    )(
        amp_mask,
        need_tiles.reshape(n_pair, need),
        amps.reshape(rows, cols),
        hh_ints,
        slot_info.reshape(owned, group).T,
        slot_count.reshape(1, owned),
        slab_pairs.T,
        occ_energy.reshape(1, -1),
        virt_energy.reshape(virt // LANES, LANES),
        integrals.reshape(owned * group, TILE * TILE),
    )
    return residual.reshape(slab, 1, home_cols)


def solution(mesh):
    return jax.shard_map(
        body,
        mesh=mesh,
        in_specs=(
            P("pair", "sum", None),
            P("sum", None),
            P("pair", None),
            P("pair", "sum", None, None),
            P("pair", "sum", None, None),
            P("pair", "sum", None),
            P(None, "sum", None),
            P(),
            P(),
            P(),
        ),
        out_specs=P(None, "sum", "pair"),
        check_vma=False,
    )
```

```python
import functools

import jax
import jax.numpy as jnp
from jax import lax
from jax.experimental import pallas as pl
from jax.experimental.pallas import tpu as pltpu
from jax.sharding import PartitionSpec as P

TILE = 64
LANES = 128
LAYERS = 4
EARLY = 0
MESH = pl.DeviceIdType.MESH
BF16 = jnp.bfloat16
F32 = jnp.float32
I32 = jnp.int32


def iota(shape, axis):
    return lax.broadcasted_iota(I32, shape, axis)


def ladder_kernel(
    dims,
    mask_in,
    need_in,
    amps_in,
    hh_in,
    info_in,
    count_in,
    slab_in,
    occ_in,
    virt_in,
    ints_in,
    out_ref,
    mask_ref,
    need_ref,
    amps_ref,
    hh_ref,
    info_ref,
    count_ref,
    slab_ref,
    occ_ref,
    virt_ref,
    pos_ref,
    plain,
    low,
    high,
    pattern,
    ints,
    weights,
    send,
    recv,
    left,
    own_part,
    part_send,
    part_recv,
    shard_ref,
    shard_hh,
    hh_all,
    relay,
    ready,
    ready_sum,
    in_sems,
    send_sems,
    recv_sems,
    part_send_sems,
    part_recv_sems,
    shard_send_sems,
    shard_recv_sems,
    relay_sems,
    column_send_sems,
    column_recv_sems,
    row_send_sems,
    row_recv_sems,
):
    n_pair, n_sum, rows, chunks, need, group, home_tiles, quads = dims
    slab = rows * n_pair
    home_pad = quads * 256
    home_cols = home_tiles * TILE
    pick_cols = need * TILE
    me = lax.axis_index("pair")
    my_sum = lax.axis_index("sum")

    width = n_pair // LAYERS
    layer, column = me // width, lax.rem(me, width)
    flip = layer // 2
    at_end = layer == flip * (LAYERS - 1)
    partner = lax.rem(me + n_pair // 2, n_pair)

    barrier = pltpu.get_barrier_semaphore()

    def greet(peer, carry):
        pl.semaphore_signal(barrier, inc=1, device_id=(peer, my_sum), device_id_type=MESH)
        return carry

    def greet_sum(peer, carry):
        pl.semaphore_signal(barrier, inc=1, device_id=(me, peer), device_id_type=MESH)
        return carry

    pairs_of_refs = (
        (mask_in, mask_ref),
        (amps_in, amps_ref),
        (need_in, need_ref),
        (hh_in, hh_ref),
        (info_in, info_ref),
        (count_in, count_ref),
        (slab_in, slab_ref),
        (occ_in, occ_ref),
        (virt_in, virt_ref),
        (ints_in, ints),
    )
    fetches = [
        pltpu.make_async_copy(src, dst, in_sems.at[at]) for at, (src, dst) in enumerate(pairs_of_refs)
    ]
    for fetch in fetches:
        fetch.start()
    lax.fori_loop(me + 1, n_pair, greet, 0)
    lax.fori_loop(my_sum + 1, n_sum, greet_sum, 0)

    @pl.when(me + my_sum > 0)
    def _():
        pl.semaphore_wait(barrier, me + my_sum)

    split = 2 * chunks // 3
    head, rest = slice(0, split * LANES), slice(split * LANES, chunks * LANES)
    shard_parts = (
        (hh_in, shard_hh),
        (amps_in.at[:, head], shard_ref.at[:, head]),
        (amps_in.at[:, rest], shard_ref.at[:, rest]),
    )

    def shard_copies():
        return [
            pltpu.make_async_remote_copy(
                src_ref=src,
                dst_ref=dst,
                send_sem=shard_send_sems.at[at],
                recv_sem=shard_recv_sems.at[at],
                device_id=(partner, my_sum),
                device_id_type=MESH,
            )
            for at, (src, dst) in enumerate(shard_parts)
        ]

    @pl.when(at_end & (flip == 1))
    def _():
        for copy in shard_copies():
            copy.start()

    def answer(peer, carry):
        @pl.when((peer >= width) | (flip == 0) | (peer == partner))
        def _():
            pl.semaphore_signal(
                ready.at[me], inc=1, device_id=(peer, my_sum), device_id_type=MESH
            )

        return carry

    def answer_sum(peer, carry):
        pl.semaphore_signal(
            ready_sum.at[my_sum], inc=1, device_id=(me, peer), device_id_type=MESH
        )
        return carry

    lax.fori_loop(0, me, answer, 0)
    lax.fori_loop(0, my_sum, answer_sum, 0)

    def wait_ready(peer):
        @pl.when(peer > me)
        def _():
            pl.semaphore_wait(ready.at[peer], 1)

    fetches[0].wait()
    fetches[1].wait()

    low_half = iota((rows, LANES), 1) < TILE
    row_at = iota((LANES, LANES), 0)
    col_at = iota((LANES, LANES), 1)
    origin = (
        (col_at & 64) + (col_at & 32) + ((col_at & 15) << 1) + ((col_at >> 4) & 1)
    )
    shuffle = jnp.where(row_at == origin, 1.0, 0.0).astype(BF16)

    def unfold(which, source, first, last):
        for chunk in range(first, last):
            keep = jnp.where(low_half, mask_ref[0, 2 * chunk], mask_ref[0, 2 * chunk + 1]).astype(F32)
            values = source[:, chunk * LANES : (chunk + 1) * LANES].astype(F32)
            plain[which, chunk] = values * keep
        moved = jnp.dot(
            plain[which, first:last].reshape((last - first) * rows, LANES).astype(BF16),
            shuffle,
            preferred_element_type=F32,
        )
        turned = pltpu.roll(moved, TILE, 1)
        count = last - first
        moved = moved.reshape(count, rows, LANES)
        turned = turned.reshape(count, rows, LANES)
        tiles = slice(2 * first, 2 * last)
        low[which, tiles] = jnp.stack([moved, turned], axis=1).reshape(2 * count, rows, LANES)
        high[which, tiles] = jnp.stack([turned, moved], axis=1).reshape(2 * count, rows, LANES)

    unfold(0, amps_ref, 0, chunks)

    fetches[2].wait()
    fetches[3].wait()

    def pack(which, peer):
        pieces = []
        for at in range(need // 2):
            first = need_ref[peer, 2 * at]
            second = need_ref[peer, 2 * at + 1]
            pieces.append(jnp.where(low_half, low[which, first], high[which, second]))
        for at in range(home_pad // LANES):
            if home_tiles % 2 == 0:
                pieces.append(plain[which, peer * (home_tiles // 2) + at])
            else:
                first = peer * home_tiles + 2 * at
                odd = lax.rem(first, 2)
                chunk = first // 2
                after = jnp.minimum(chunk + 1, chunks - 1)
                here = plain[which, chunk]
                joined = jnp.where(
                    low_half, pltpu.roll(here, TILE, 1), pltpu.roll(plain[which, after], TILE, 1)
                )
                pieces.append(jnp.where(jnp.broadcast_to(odd == 1, here.shape), joined, here))
        return jnp.concatenate(pieces, axis=1).astype(BF16)

    def place(to_layer, turn):
        ahead = jnp.where(turn == 0, 0, 1 + lax.rem(column + turn, width - 1))
        beside = lax.rem(column + turn + jnp.where(to_layer == layer, 1, 0), width)
        return to_layer * width + jnp.where(to_layer == 0, ahead, beside)

    def peer_at(step):
        own = width - 1
        low_step, high_step = step - width - own, step - 2 * width
        up_layer = jnp.where((low_step >= 1) & (low_step < width + 1), 3, 2)
        up_turn = jnp.where(low_step < 1, low_step, jnp.where(up_layer == 3, low_step - 1, low_step - width))
        low_layer = jnp.where(step < width, 0, jnp.where(low_step < 0, 1, up_layer))
        low_turn = jnp.where(step < width, step, jnp.where(low_step < 0, step - width, up_turn))
        high_layer = jnp.where(high_step < 0, step // width, jnp.where(high_step < own, 2, 3))
        high_turn = jnp.where(
            high_step < 0, lax.rem(step, width), jnp.where(high_step < own, high_step, high_step - own)
        )
        end_layer = jnp.where(step < own, layer, 1 + flip)
        end_turn = jnp.where(step < own, step, step - own)
        to_layer = jnp.where(at_end, end_layer, jnp.where(flip == 0, low_layer, high_layer))
        turn = jnp.where(at_end, end_turn, jnp.where(flip == 0, low_turn, high_turn))
        own_place = layer * width + lax.rem(column + turn + 1, width)
        return jnp.where(to_layer == layer, own_place, place(to_layer, turn))

    def block_copy(peer):
        return pltpu.make_async_remote_copy(
            src_ref=send.at[peer],
            dst_ref=recv.at[me],
            send_sem=send_sems.at[peer],
            recv_sem=recv_sems.at[me],
            device_id=(peer, my_sum),
            device_id_type=MESH,
        )

    def column_copy(peer):
        return pltpu.make_async_remote_copy(
            src_ref=hh_ref,
            dst_ref=hh_all.at[layer, column],
            send_sem=column_send_sems.at[peer // width],
            recv_sem=column_recv_sems.at[layer],
            device_id=(peer, my_sum),
            device_id_type=MESH,
        )

    far_layer = partner // width

    def column_relay():
        return pltpu.make_async_remote_copy(
            src_ref=shard_hh,
            dst_ref=hh_all.at[far_layer, column],
            send_sem=column_send_sems.at[layer],
            recv_sem=column_recv_sems.at[far_layer],
            device_id=(flip * (LAYERS - 1) * width + column, my_sum),
            device_id_type=MESH,
        )

    def row_copy(place):
        return pltpu.make_async_remote_copy(
            src_ref=hh_all.at[:, column],
            dst_ref=hh_all.at[:, column],
            send_sem=row_send_sems.at[place],
            recv_sem=row_recv_sems.at[column],
            device_id=(layer * width + place, my_sum),
            device_id_type=MESH,
        )

    def column_arrival(source):
        return pltpu.make_async_remote_copy(
            src_ref=hh_ref,
            dst_ref=hh_all.at[source, column],
            send_sem=column_send_sems.at[source],
            recv_sem=column_recv_sems.at[source],
            device_id=(source * width + column, my_sum),
            device_id_type=MESH,
        )

    def row_arrival(place):
        return pltpu.make_async_remote_copy(
            src_ref=hh_all.at[:, place],
            dst_ref=hh_all.at[:, place],
            send_sem=row_send_sems.at[place],
            recv_sem=row_recv_sems.at[place],
            device_id=(layer * width + place, my_sum),
            device_id_type=MESH,
        )

    hh_all[layer, column] = hh_ref[...]

    def send_step(step, carry):
        peer = peer_at(step)
        send[peer] = pack(0, peer)
        wait_ready(peer)
        block_copy(peer).start()

        @pl.when(lax.rem(peer, width) == column)
        def _():
            column_copy(peer).start()

        @pl.when(at_end & (flip == 0) & (step == width - 2 + EARLY))
        def _():
            wait_ready(partner)
            for copy in shard_copies():
                copy.start()

        return carry

    directs = jnp.where(at_end, n_pair // 2 - 1, n_pair - 1)
    later = jnp.where(flip == 0, 2 * width - 1, 0)
    soon = jnp.where(at_end, directs, directs - later)
    lax.fori_loop(0, soon, send_step, 0)
    recv[me] = pack(0, me)

    spread_rows = need * 16
    spread_cols = 16 * group
    row_at = iota((spread_rows, spread_cols), 0)
    col_at = iota((spread_rows, spread_cols), 1)
    pattern[...] = jnp.where((row_at & 15) == col_at // group, row_at >> 4, -1).astype(F32)
    pair_low = iota((spread_rows, LANES), 1) < TILE
    for fetch in fetches[4:]:
        fetch.wait()
    live = iota(info_ref.shape, 0) < count_ref[...]
    positions = jnp.where(live, info_ref[...], -2).astype(F32).astype(BF16)
    repeat = jnp.where(
        iota((group, spread_cols), 0) == lax.rem(iota((group, spread_cols), 1), group), 1.0, 0.0
    ).astype(BF16)
    pos_ref[...] = lax.dot_general(
        positions, repeat, (((0,), (0,)), ((), ())), preferred_element_type=F32
    )

    def spread(tile):
        picked = jnp.where(pattern[...] == pos_ref[pl.ds(tile, 1), :], 1.0, 0.0).astype(BF16)
        base = pl.multiple_of(tile * group, group)
        halves = []
        for half in range(2):
            stack = [
                ints[pl.ds(base, group), (half * 16 + k) * LANES : (half * 16 + k + 1) * LANES]
                for k in range(16)
            ]
            halves.append(jnp.concatenate(stack, axis=0))
        stacked = jnp.concatenate(halves, axis=1)
        return jnp.dot(picked, stacked, preferred_element_type=F32)

    def spread_quad(at, carry):
        dest = at // quads
        quad = lax.rem(at, quads)
        first = dest * home_tiles + quad * 4
        for pair in range(2):
            lone = quads == 1 and 2 * pair + 1 >= home_tiles
            a = spread(first + 2 * pair)
            b = None if lone else spread(first + 2 * pair + 1)
            for half in range(2):
                a_half = a[:, half * LANES : (half + 1) * LANES]
                b_half = jnp.zeros_like(a_half) if lone else b[:, half * LANES : (half + 1) * LANES]
                even = jnp.where(pair_low, a_half, pltpu.roll(b_half, TILE, 1)).astype(BF16)
                odd = jnp.where(pair_low, pltpu.roll(a_half, TILE, 1), b_half).astype(BF16)
                cols = slice(pair * LANES, (pair + 1) * LANES)
                weights[dest, quad, :, 2 * half, :, cols] = even.reshape(need, 16, LANES)
                weights[dest, quad, :, 2 * half + 1, :, cols] = odd.reshape(need, 16, LANES)
        return carry


    some = n_sum * quads // 2
    lax.fori_loop(0, some, spread_quad, 0)
    lax.fori_loop(soon, directs, send_step, 0)
    lax.fori_loop(some, n_sum * quads, spread_quad, 0)

    def relay_copy(peer):
        slot = lax.rem(peer, n_pair // 2)
        return pltpu.make_async_remote_copy(
            src_ref=relay.at[slot],
            dst_ref=recv.at[partner],
            send_sem=relay_sems.at[slot],
            recv_sem=recv_sems.at[partner],
            device_id=(peer, my_sum),
            device_id_type=MESH,
        )

    def relay_peer(step):
        turn = lax.rem(step, 2)
        near = jnp.where(flip == 0, turn, 1 - turn)
        return place(flip * 2 + near, step // 2)

    @pl.when(jnp.logical_not(at_end))
    def _():
        copies = shard_copies()
        copies[0].wait_recv()
        hh_all[far_layer, column] = shard_hh[...]
        column_relay().start()
        copies[1].wait_recv()
        unfold(1, shard_ref, 0, split)
        copies[2].wait_recv()
        unfold(1, shard_ref, split, chunks)

        def relay_step(step, carry):
            peer = relay_peer(step)
            block = pack(1, peer)

            @pl.when(peer == me)
            def _():
                recv[partner] = block

            @pl.when(peer != me)
            def _():
                relay[lax.rem(peer, n_pair // 2)] = block
                relay_copy(peer).start()

            return carry

        lax.fori_loop(0, n_pair // 2, relay_step, 0)

    def column_step(source, carry):
        @pl.when((source != layer) & (at_end | (source != far_layer_of_end)))
        def _():
            column_arrival(source).wait_recv()

        return carry

    def row_step(step, carry):
        row_copy(lax.rem(column + step, width)).start()
        return carry

    far_layer_of_end = (1 - flip) * (LAYERS - 1)
    lax.fori_loop(0, LAYERS, column_step, 0)
    lax.fori_loop(1, width, row_step, 0)

    occ_at = iota((slab, occ_ref.shape[1]), 1).astype(F32)
    occ_row = occ_ref[...]
    orbitals = jnp.concatenate([slab_ref[...].astype(F32), jnp.zeros((6, slab), F32)], axis=0).T
    occ_i = jnp.sum(jnp.where(orbitals[:, 0:1] == occ_at, occ_row, 0.0), axis=1, keepdims=True)
    occ_j = jnp.sum(jnp.where(orbitals[:, 1:2] == occ_at, occ_row, 0.0), axis=1, keepdims=True)
    occ_pair = occ_i + occ_j

    virt_count = virt_ref.shape[0] * LANES
    start = me * home_cols
    first_at = my_sum * (chunks * LANES // virt_count) + start // virt_count
    lane = iota((1, LANES), 1)
    first_virt = jnp.sum(
        jnp.where(lane == lax.rem(first_at, LANES), virt_ref[pl.ds(first_at // LANES, 1), :], 0.0),
        axis=1,
        keepdims=True,
    )
    pieces = []
    for at in range(home_pad // LANES):
        row = (lax.rem(start, virt_count) + at * LANES) // LANES
        here = virt_ref[pl.ds(row, 1), :]
        if home_tiles % 2:
            after = virt_ref[pl.ds(jnp.minimum(row + 1, virt_ref.shape[0] - 1), 1), :]
            joined = jnp.where(lane < TILE, pltpu.roll(here, TILE, 1), pltpu.roll(after, TILE, 1))
            odd = lax.rem(me * home_tiles, 2)
            here = jnp.where(jnp.broadcast_to(odd == 1, here.shape), joined, here)
        pieces.append(here)
    pair_row = first_virt + jnp.concatenate(pieces, axis=1)

    def arrival(peer):
        return pltpu.make_async_remote_copy(
            src_ref=send.at[peer],
            dst_ref=recv.at[peer],
            send_sem=send_sems.at[peer],
            recv_sem=recv_sems.at[peer],
            device_id=(peer, my_sum),
            device_id_type=MESH,
        )

    reach = n_pair // 2
    half_rows = reach * rows
    halves = (flip, 1 - flip)

    def take_half(phase):
        def take_step(step, carry):
            first = halves[phase] * reach + 2 * step
            for side in range(2):
                peer = first + side
                mine = jnp.logical_not(at_end) & (peer == partner)

                @pl.when((peer != me) & jnp.logical_not(mine))
                def _():
                    arrival(peer).wait_recv()

            both = recv[pl.ds(first, 2), :, :pick_cols].astype(F32).reshape(2 * rows, pick_cols)
            at = pl.multiple_of(step * 2 * rows, 2 * rows)
            left[phase, pl.ds(at, 2 * rows), :] = both.astype(BF16)
            return carry

        lax.fori_loop(0, reach // 2, take_step, 0)

    def part_of(phase, dest):
        terms = []
        for quad in range(quads):
            right = weights[dest, quad].reshape(need * TILE, 256)
            terms.append(jnp.dot(left[phase], right, preferred_element_type=F32))
        return jnp.concatenate(terms, axis=1).astype(BF16)

    def part_copy(phase, source, target):
        return pltpu.make_async_remote_copy(
            src_ref=part_send.at[phase, target],
            dst_ref=part_recv.at[phase, source],
            send_sem=part_send_sems.at[phase, target],
            recv_sem=part_recv_sems.at[phase, source],
            device_id=(me, target),
            device_id_type=MESH,
        )

    def other_sums():
        return [lax.rem(my_sum + step, n_sum) for step in range(1, n_sum)]

    take_half(0)
    for dest in other_sums():
        part_send[0, dest] = part_of(0, dest)

        @pl.when(dest > my_sum)
        def _():
            pl.semaphore_wait(ready_sum.at[dest], 1)

        part_copy(0, my_sum, dest).start()
    own_part[...] = part_of(0, my_sum)

    take_half(1)
    for dest in other_sums():
        part_send[1, dest] = part_of(1, dest)
        part_copy(1, my_sum, dest).start()
    home = recv[:, :, pick_cols : pick_cols + home_pad].astype(F32).reshape(slab, home_pad)
    home = home.astype(BF16)

    def row_take(step, carry):
        row_arrival(lax.rem(column + step, width)).wait_recv()
        return carry

    lax.fori_loop(1, width, row_take, 0)
    totals = []
    for phase in range(2):
        own = own_part[...] if phase == 0 else part_of(1, my_sum)
        lines = pl.ds(halves[phase] * reach, reach)
        here = recv[lines, :, pick_cols : pick_cols + home_pad].astype(F32)
        hh_rows = hh_all[pl.ds(halves[phase] * (LAYERS // 2), LAYERS // 2)].astype(F32)
        occ_rows = jnp.where(flip == phase, occ_pair[:half_rows], occ_pair[half_rows:])
        total = (pair_row - occ_rows) * here.reshape(half_rows, home_pad)
        total = total + jnp.dot(
            hh_rows.reshape(half_rows, slab).astype(BF16), home, preferred_element_type=F32
        )
        totals.append(total + own.astype(F32))
    for phase in range(2):
        total = totals[phase]
        for dest in other_sums():
            part_copy(phase, dest, dest).wait()
            total = total + part_recv[phase, dest].astype(F32)
        if out_ref.shape[1] == LANES:
            lines = home_cols // LANES
            base = halves[phase] * (half_rows * lines)
            for at in range(lines):
                out_ref[pl.ds(base + at, half_rows, stride=lines), :] = total[
                    :, at * LANES : (at + 1) * LANES
                ]
        else:
            base = pl.multiple_of(halves[phase] * half_rows, half_rows)
            out_ref[pl.ds(base, half_rows), :] = total[:, :home_cols]

    def sent_step(step, carry):
        block_copy(peer_at(step)).wait_send()
        return carry

    lax.fori_loop(0, directs, sent_step, 0)

    def row_sent(step, carry):
        row_copy(lax.rem(column + step, width)).wait_send()
        return carry

    lax.fori_loop(1, width, row_sent, 0)

    @pl.when(at_end)
    def _():
        column_copy((1 + flip) * width + column).wait_send()

    @pl.when(jnp.logical_not(at_end))
    def _():
        column_relay().wait_send()

        def column_sent(target, carry):
            @pl.when(target != layer)
            def _():
                column_copy(target * width + column).wait_send()

            return carry

        lax.fori_loop(0, LAYERS, column_sent, 0)

    def relayed_step(step, carry):
        peer = relay_peer(step)

        @pl.when(peer != me)
        def _():
            relay_copy(peer).wait_send()

        return carry

    @pl.when(jnp.logical_not(at_end))
    def _():
        lax.fori_loop(0, n_pair // 2, relayed_step, 0)

    @pl.when(at_end)
    def _():
        for copy in shard_copies():
            copy.wait_send()


def body(
    amps,
    amp_mask,
    hh_ints,
    integrals,
    slot_info,
    slot_count,
    need_tiles,
    slab_pairs,
    occ_energy,
    virt_energy,
):
    n_pair = lax.axis_size("pair")
    n_sum = lax.axis_size("sum")
    rows = amps.shape[0]
    cols = amps.shape[2]
    chunks = cols // LANES
    home_cols = cols // n_pair
    home_tiles = home_cols // TILE
    need = need_tiles.shape[2]
    owned, group = slot_info.shape[2], slot_info.shape[3]
    slab = rows * n_pair
    virt = virt_energy.shape[0]
    assert home_cols % TILE == 0 and virt % home_cols == 0 and cols % LANES == 0
    assert home_tiles % 4 == 0 or home_tiles < 4
    quads = -(-home_tiles // 4)
    home_pad = quads * 256
    block_cols = need * TILE + home_pad

    out_shape = (slab, home_cols) if home_cols % LANES else (slab * home_cols // LANES, LANES)

    vmem = pl.BlockSpec(memory_space=pltpu.VMEM)
    anywhere = pl.BlockSpec(memory_space=pltpu.HBM)
    dims = (n_pair, n_sum, rows, chunks, need, group, home_tiles, quads)
    residual = pl.pallas_call(
        functools.partial(ladder_kernel, dims),
        out_shape=pltpu.VMEM(out_shape, F32),
        in_specs=[anywhere] * 10,
        out_specs=vmem,
        scratch_shapes=[
            pltpu.SMEM(amp_mask.shape, I32),
            pltpu.SMEM((n_pair, need), I32),
            pltpu.VMEM((rows, cols), BF16),
            pltpu.VMEM(hh_ints.shape, BF16),
            pltpu.VMEM((group, owned), I32),
            pltpu.VMEM((1, owned), I32),
            pltpu.VMEM((2, slab), I32),
            pltpu.VMEM((1, occ_energy.shape[0]), F32),
            pltpu.VMEM((virt // LANES, LANES), F32),
            pltpu.VMEM((owned, 16 * group), F32),
            pltpu.VMEM((2, chunks, rows, LANES), F32),
            pltpu.VMEM((2, 2 * chunks, rows, LANES), F32),
            pltpu.VMEM((2, 2 * chunks, rows, LANES), F32),
            pltpu.VMEM((need * 16, 16 * group), F32),
            pltpu.VMEM((owned * group, TILE * TILE), BF16),
            pltpu.VMEM((n_sum, quads, need, 4, 16, 256), BF16),
            pltpu.VMEM((n_pair, rows, block_cols), BF16),
            pltpu.VMEM((n_pair, rows, block_cols), BF16),
            pltpu.VMEM((2, slab // 2, need * TILE), BF16),
            pltpu.VMEM((slab // 2, home_pad), BF16),
            pltpu.VMEM((2, n_sum, slab // 2, home_pad), BF16),
            pltpu.VMEM((2, n_sum, slab // 2, home_pad), BF16),
            pltpu.VMEM((rows, cols), BF16),
            pltpu.VMEM((rows, slab), BF16),
            pltpu.VMEM((LAYERS, n_pair // LAYERS, rows, slab), BF16),
            pltpu.VMEM((n_pair // 2, rows, block_cols), BF16),
            pltpu.SemaphoreType.REGULAR((n_pair,)),
            pltpu.SemaphoreType.REGULAR((n_sum,)),
            pltpu.SemaphoreType.DMA((10,)),
            pltpu.SemaphoreType.DMA((n_pair,)),
            pltpu.SemaphoreType.DMA((n_pair,)),
            pltpu.SemaphoreType.DMA((2, n_sum)),
            pltpu.SemaphoreType.DMA((2, n_sum)),
            pltpu.SemaphoreType.DMA((3,)),
            pltpu.SemaphoreType.DMA((3,)),
            pltpu.SemaphoreType.DMA((n_pair // 2,)),
            pltpu.SemaphoreType.DMA((LAYERS,)),
            pltpu.SemaphoreType.DMA((LAYERS,)),
            pltpu.SemaphoreType.DMA((n_pair // LAYERS,)),
            pltpu.SemaphoreType.DMA((n_pair // LAYERS,)),
        ],
        compiler_params=pltpu.CompilerParams(
            collective_id=0, has_side_effects=True, vmem_limit_bytes=56 * 1024 * 1024
        ),
    )(
        amp_mask,
        need_tiles.reshape(n_pair, need),
        amps.reshape(rows, cols),
        hh_ints,
        slot_info.reshape(owned, group).T,
        slot_count.reshape(1, owned),
        slab_pairs.T,
        occ_energy.reshape(1, -1),
        virt_energy.reshape(virt // LANES, LANES),
        integrals.reshape(owned * group, TILE * TILE),
    )
    return residual.reshape(slab, 1, home_cols)


def solution(mesh):
    return jax.shard_map(
        body,
        mesh=mesh,
        in_specs=(
            P("pair", "sum", None),
            P("sum", None),
            P("pair", None),
            P("pair", "sum", None, None),
            P("pair", "sum", None, None),
            P("pair", "sum", None),
            P(None, "sum", None),
            P(),
            P(),
            P(),
        ),
        out_specs=P(None, "sum", "pair"),
        check_vma=False,
    )
```

```python
import functools

import jax
import jax.numpy as jnp
from jax import lax
from jax.experimental import pallas as pl
from jax.experimental.pallas import tpu as pltpu
from jax.sharding import PartitionSpec as P

TILE = 64
LANES = 128
LAYERS = 4
EARLY = 0
MESH = pl.DeviceIdType.MESH
BF16 = jnp.bfloat16
F32 = jnp.float32
I32 = jnp.int32


def iota(shape, axis):
    return lax.broadcasted_iota(I32, shape, axis)


def ladder_kernel(
    dims,
    mask_in,
    need_in,
    amps_in,
    hh_in,
    info_in,
    count_in,
    slab_in,
    occ_in,
    virt_in,
    ints_in,
    out_ref,
    mask_ref,
    need_ref,
    amps_ref,
    hh_ref,
    info_ref,
    count_ref,
    slab_ref,
    occ_ref,
    virt_ref,
    pos_ref,
    plain,
    low,
    high,
    pattern,
    ints,
    weights,
    send,
    recv,
    left,
    own_part,
    part_send,
    part_recv,
    shard_ref,
    shard_hh,
    hh_all,
    relay,
    ready,
    ready_sum,
    in_sems,
    send_sems,
    recv_sems,
    part_send_sems,
    part_recv_sems,
    shard_send_sems,
    shard_recv_sems,
    relay_sems,
    column_send_sems,
    column_recv_sems,
    row_send_sems,
    row_recv_sems,
):
    n_pair, n_sum, rows, chunks, need, group, home_tiles, quads = dims
    slab = rows * n_pair
    home_pad = quads * 256
    home_cols = home_tiles * TILE
    pick_cols = need * TILE
    me = lax.axis_index("pair")
    my_sum = lax.axis_index("sum")

    width = n_pair // LAYERS
    layer, column = me // width, lax.rem(me, width)
    flip = layer // 2
    at_end = layer == flip * (LAYERS - 1)
    partner = lax.rem(me + n_pair // 2, n_pair)

    barrier = pltpu.get_barrier_semaphore()

    def greet(peer, carry):
        pl.semaphore_signal(barrier, inc=1, device_id=(peer, my_sum), device_id_type=MESH)
        return carry

    def greet_sum(peer, carry):
        pl.semaphore_signal(barrier, inc=1, device_id=(me, peer), device_id_type=MESH)
        return carry

    pairs_of_refs = (
        (mask_in, mask_ref),
        (amps_in, amps_ref),
        (need_in, need_ref),
        (hh_in, hh_ref),
        (info_in, info_ref),
        (count_in, count_ref),
        (slab_in, slab_ref),
        (occ_in, occ_ref),
        (virt_in, virt_ref),
        (ints_in, ints),
    )
    fetches = [
        pltpu.make_async_copy(src, dst, in_sems.at[at]) for at, (src, dst) in enumerate(pairs_of_refs)
    ]
    for fetch in fetches:
        fetch.start()
    lax.fori_loop(me + 1, n_pair, greet, 0)
    lax.fori_loop(my_sum + 1, n_sum, greet_sum, 0)

    @pl.when(me + my_sum > 0)
    def _():
        pl.semaphore_wait(barrier, me + my_sum)

    split = 2 * chunks // 3
    head, rest = slice(0, split * LANES), slice(split * LANES, chunks * LANES)
    shard_parts = (
        (hh_in, shard_hh),
        (amps_in.at[:, head], shard_ref.at[:, head]),
        (amps_in.at[:, rest], shard_ref.at[:, rest]),
    )

    def shard_copies():
        return [
            pltpu.make_async_remote_copy(
                src_ref=src,
                dst_ref=dst,
                send_sem=shard_send_sems.at[at],
                recv_sem=shard_recv_sems.at[at],
                device_id=(partner, my_sum),
                device_id_type=MESH,
            )
            for at, (src, dst) in enumerate(shard_parts)
        ]

    @pl.when(at_end & (flip == 1))
    def _():
        for copy in shard_copies():
            copy.start()

    def answer(peer, carry):
        @pl.when((peer >= width) | (flip == 0) | (peer == partner))
        def _():
            pl.semaphore_signal(
                ready.at[me], inc=1, device_id=(peer, my_sum), device_id_type=MESH
            )

        return carry

    def answer_sum(peer, carry):
        pl.semaphore_signal(
            ready_sum.at[my_sum], inc=1, device_id=(me, peer), device_id_type=MESH
        )
        return carry

    lax.fori_loop(0, me, answer, 0)
    lax.fori_loop(0, my_sum, answer_sum, 0)

    def wait_ready(peer):
        @pl.when(peer > me)
        def _():
            pl.semaphore_wait(ready.at[peer], 1)

    fetches[0].wait()
    fetches[1].wait()

    low_half = iota((rows, LANES), 1) < TILE
    row_at = iota((LANES, LANES), 0)
    col_at = iota((LANES, LANES), 1)
    origin = (
        (col_at & 64) + (col_at & 32) + ((col_at & 15) << 1) + ((col_at >> 4) & 1)
    )
    shuffle = jnp.where(row_at == origin, 1.0, 0.0).astype(BF16)

    def unfold(which, source, first, last):
        for chunk in range(first, last):
            keep = jnp.where(low_half, mask_ref[0, 2 * chunk], mask_ref[0, 2 * chunk + 1]).astype(F32)
            values = source[:, chunk * LANES : (chunk + 1) * LANES].astype(F32)
            plain[which, chunk] = values * keep
        moved = jnp.dot(
            plain[which, first:last].reshape((last - first) * rows, LANES).astype(BF16),
            shuffle,
            preferred_element_type=F32,
        )
        turned = pltpu.roll(moved, TILE, 1)
        count = last - first
        moved = moved.reshape(count, rows, LANES)
        turned = turned.reshape(count, rows, LANES)
        tiles = slice(2 * first, 2 * last)
        low[which, tiles] = jnp.stack([moved, turned], axis=1).reshape(2 * count, rows, LANES)
        high[which, tiles] = jnp.stack([turned, moved], axis=1).reshape(2 * count, rows, LANES)

    unfold(0, amps_ref, 0, chunks)

    fetches[2].wait()
    fetches[3].wait()

    def pack(which, peer):
        pieces = []
        for at in range(need // 2):
            first = need_ref[peer, 2 * at]
            second = need_ref[peer, 2 * at + 1]
            pieces.append(jnp.where(low_half, low[which, first], high[which, second]))
        for at in range(home_pad // LANES):
            if home_tiles % 2 == 0:
                pieces.append(plain[which, peer * (home_tiles // 2) + at])
            else:
                first = peer * home_tiles + 2 * at
                odd = lax.rem(first, 2)
                chunk = first // 2
                after = jnp.minimum(chunk + 1, chunks - 1)
                here = plain[which, chunk]
                joined = jnp.where(
                    low_half, pltpu.roll(here, TILE, 1), pltpu.roll(plain[which, after], TILE, 1)
                )
                pieces.append(jnp.where(jnp.broadcast_to(odd == 1, here.shape), joined, here))
        return jnp.concatenate(pieces, axis=1).astype(BF16)

    def place(to_layer, turn):
        ahead = jnp.where(turn == 0, 0, 1 + lax.rem(column + turn, width - 1))
        beside = lax.rem(column + turn + jnp.where(to_layer == layer, 1, 0), width)
        return to_layer * width + jnp.where(to_layer == 0, ahead, beside)

    def peer_at(step):
        own = width - 1
        low_step, high_step = step - width - own, step - 2 * width
        up_layer = jnp.where((low_step >= 1) & (low_step < width + 1), 3, 2)
        up_turn = jnp.where(low_step < 1, low_step, jnp.where(up_layer == 3, low_step - 1, low_step - width))
        low_layer = jnp.where(step < width, 0, jnp.where(low_step < 0, 1, up_layer))
        low_turn = jnp.where(step < width, step, jnp.where(low_step < 0, step - width, up_turn))
        high_layer = jnp.where(high_step < 0, step // width, jnp.where(high_step < own, 2, 3))
        high_turn = jnp.where(
            high_step < 0, lax.rem(step, width), jnp.where(high_step < own, high_step, high_step - own)
        )
        end_layer = jnp.where(step < own, layer, 1 + flip)
        end_turn = jnp.where(step < own, step, step - own)
        to_layer = jnp.where(at_end, end_layer, jnp.where(flip == 0, low_layer, high_layer))
        turn = jnp.where(at_end, end_turn, jnp.where(flip == 0, low_turn, high_turn))
        own_place = layer * width + lax.rem(column + turn + 1, width)
        return jnp.where(to_layer == layer, own_place, place(to_layer, turn))

    parts = (slice(0, pick_cols), slice(pick_cols, pick_cols + home_pad))

    def split_home(peer):
        return peer != 0

    def block_copy(peer, part):
        return pltpu.make_async_remote_copy(
            src_ref=send.at[peer, :, parts[part]],
            dst_ref=recv.at[me, :, parts[part]],
            send_sem=send_sems.at[part, peer],
            recv_sem=recv_sems.at[part, me],
            device_id=(peer, my_sum),
            device_id_type=MESH,
        )

    def column_copy(peer):
        return pltpu.make_async_remote_copy(
            src_ref=hh_ref,
            dst_ref=hh_all.at[layer, column],
            send_sem=column_send_sems.at[peer // width],
            recv_sem=column_recv_sems.at[layer],
            device_id=(peer, my_sum),
            device_id_type=MESH,
        )

    far_layer = partner // width

    def column_relay():
        return pltpu.make_async_remote_copy(
            src_ref=shard_hh,
            dst_ref=hh_all.at[far_layer, column],
            send_sem=column_send_sems.at[layer],
            recv_sem=column_recv_sems.at[far_layer],
            device_id=(flip * (LAYERS - 1) * width + column, my_sum),
            device_id_type=MESH,
        )

    def row_copy(place):
        return pltpu.make_async_remote_copy(
            src_ref=hh_all.at[:, column],
            dst_ref=hh_all.at[:, column],
            send_sem=row_send_sems.at[place],
            recv_sem=row_recv_sems.at[column],
            device_id=(layer * width + place, my_sum),
            device_id_type=MESH,
        )

    def column_arrival(source):
        return pltpu.make_async_remote_copy(
            src_ref=hh_ref,
            dst_ref=hh_all.at[source, column],
            send_sem=column_send_sems.at[source],
            recv_sem=column_recv_sems.at[source],
            device_id=(source * width + column, my_sum),
            device_id_type=MESH,
        )

    def row_arrival(place):
        return pltpu.make_async_remote_copy(
            src_ref=hh_all.at[:, place],
            dst_ref=hh_all.at[:, place],
            send_sem=row_send_sems.at[place],
            recv_sem=row_recv_sems.at[place],
            device_id=(layer * width + place, my_sum),
            device_id_type=MESH,
        )

    hh_all[layer, column] = hh_ref[...]

    def send_step(step, carry):
        peer = peer_at(step)
        send[peer] = pack(0, peer)
        wait_ready(peer)
        block_copy(peer, 0).start()

        @pl.when(jnp.logical_not(split_home(peer)))
        def _():
            block_copy(peer, 1).start()

        @pl.when(lax.rem(peer, width) == column)
        def _():
            column_copy(peer).start()

        @pl.when(at_end & (flip == 0) & (step == width - 2 + EARLY))
        def _():
            wait_ready(partner)
            for copy in shard_copies():
                copy.start()

        return carry

    directs = jnp.where(at_end, n_pair // 2 - 1, n_pair - 1)
    later = jnp.where(flip == 0, 2 * width - 1, 0)
    soon = jnp.where(at_end, directs, directs - later)
    lax.fori_loop(0, soon, send_step, 0)
    recv[me] = pack(0, me)

    spread_rows = need * 16
    spread_cols = 16 * group
    row_at = iota((spread_rows, spread_cols), 0)
    col_at = iota((spread_rows, spread_cols), 1)
    pattern[...] = jnp.where((row_at & 15) == col_at // group, row_at >> 4, -1).astype(F32)
    pair_low = iota((spread_rows, LANES), 1) < TILE
    for fetch in fetches[4:]:
        fetch.wait()
    live = iota(info_ref.shape, 0) < count_ref[...]
    positions = jnp.where(live, info_ref[...], -2).astype(F32).astype(BF16)
    repeat = jnp.where(
        iota((group, spread_cols), 0) == lax.rem(iota((group, spread_cols), 1), group), 1.0, 0.0
    ).astype(BF16)
    pos_ref[...] = lax.dot_general(
        positions, repeat, (((0,), (0,)), ((), ())), preferred_element_type=F32
    )

    def spread(tile):
        picked = jnp.where(pattern[...] == pos_ref[pl.ds(tile, 1), :], 1.0, 0.0).astype(BF16)
        base = pl.multiple_of(tile * group, group)
        halves = []
        for half in range(2):
            stack = [
                ints[pl.ds(base, group), (half * 16 + k) * LANES : (half * 16 + k + 1) * LANES]
                for k in range(16)
            ]
            halves.append(jnp.concatenate(stack, axis=0))
        stacked = jnp.concatenate(halves, axis=1)
        return jnp.dot(picked, stacked, preferred_element_type=F32)

    def spread_quad(at, carry):
        dest = at // quads
        quad = lax.rem(at, quads)
        first = dest * home_tiles + quad * 4
        for pair in range(2):
            lone = quads == 1 and 2 * pair + 1 >= home_tiles
            a = spread(first + 2 * pair)
            b = None if lone else spread(first + 2 * pair + 1)
            for half in range(2):
                a_half = a[:, half * LANES : (half + 1) * LANES]
                b_half = jnp.zeros_like(a_half) if lone else b[:, half * LANES : (half + 1) * LANES]
                even = jnp.where(pair_low, a_half, pltpu.roll(b_half, TILE, 1)).astype(BF16)
                odd = jnp.where(pair_low, pltpu.roll(a_half, TILE, 1), b_half).astype(BF16)
                cols = slice(pair * LANES, (pair + 1) * LANES)
                weights[dest, quad, :, 2 * half, :, cols] = even.reshape(need, 16, LANES)
                weights[dest, quad, :, 2 * half + 1, :, cols] = odd.reshape(need, 16, LANES)
        return carry


    some = n_sum * quads // 2
    lax.fori_loop(0, some, spread_quad, 0)
    lax.fori_loop(soon, directs, send_step, 0)

    def home_step(step, carry):
        @pl.when(split_home(peer_at(step)))
        def _():
            block_copy(peer_at(step), 1).start()

        return carry

    lax.fori_loop(0, directs, home_step, 0)
    lax.fori_loop(some, n_sum * quads, spread_quad, 0)

    def relay_copy(peer, part):
        slot = lax.rem(peer, n_pair // 2)
        return pltpu.make_async_remote_copy(
            src_ref=relay.at[slot, :, parts[part]],
            dst_ref=recv.at[partner, :, parts[part]],
            send_sem=relay_sems.at[part, slot],
            recv_sem=recv_sems.at[part, partner],
            device_id=(peer, my_sum),
            device_id_type=MESH,
        )

    def relay_peer(step):
        turn = lax.rem(step, 2)
        near = jnp.where(flip == 0, turn, 1 - turn)
        return place(flip * 2 + near, step // 2)

    @pl.when(jnp.logical_not(at_end))
    def _():
        copies = shard_copies()
        copies[0].wait_recv()
        hh_all[far_layer, column] = shard_hh[...]
        column_relay().start()
        copies[1].wait_recv()
        unfold(1, shard_ref, 0, split)
        copies[2].wait_recv()
        unfold(1, shard_ref, split, chunks)

        def relay_step(step, carry):
            peer = relay_peer(step)
            block = pack(1, peer)

            @pl.when(peer == me)
            def _():
                recv[partner] = block

            @pl.when(peer != me)
            def _():
                relay[lax.rem(peer, n_pair // 2)] = block
                relay_copy(peer, 0).start()

            @pl.when((peer != me) & (peer == 0))
            def _():
                relay_copy(peer, 1).start()

            return carry

        lax.fori_loop(0, n_pair // 2, relay_step, 0)

        def relay_home_step(step, carry):
            peer = relay_peer(step)

            @pl.when((peer != me) & jnp.logical_not(peer == 0))
            def _():
                relay_copy(peer, 1).start()

            return carry

        lax.fori_loop(0, n_pair // 2, relay_home_step, 0)

    def column_step(source, carry):
        @pl.when((source != layer) & (at_end | (source != far_layer_of_end)))
        def _():
            column_arrival(source).wait_recv()

        return carry

    def row_step(step, carry):
        row_copy(lax.rem(column + step, width)).start()
        return carry

    far_layer_of_end = (1 - flip) * (LAYERS - 1)
    lax.fori_loop(0, LAYERS, column_step, 0)
    lax.fori_loop(1, width, row_step, 0)

    occ_at = iota((slab, occ_ref.shape[1]), 1).astype(F32)
    occ_row = occ_ref[...]
    orbitals = jnp.concatenate([slab_ref[...].astype(F32), jnp.zeros((6, slab), F32)], axis=0).T
    occ_i = jnp.sum(jnp.where(orbitals[:, 0:1] == occ_at, occ_row, 0.0), axis=1, keepdims=True)
    occ_j = jnp.sum(jnp.where(orbitals[:, 1:2] == occ_at, occ_row, 0.0), axis=1, keepdims=True)
    occ_pair = occ_i + occ_j

    virt_count = virt_ref.shape[0] * LANES
    start = me * home_cols
    first_at = my_sum * (chunks * LANES // virt_count) + start // virt_count
    lane = iota((1, LANES), 1)
    first_virt = jnp.sum(
        jnp.where(lane == lax.rem(first_at, LANES), virt_ref[pl.ds(first_at // LANES, 1), :], 0.0),
        axis=1,
        keepdims=True,
    )
    pieces = []
    for at in range(home_pad // LANES):
        row = (lax.rem(start, virt_count) + at * LANES) // LANES
        here = virt_ref[pl.ds(row, 1), :]
        if home_tiles % 2:
            after = virt_ref[pl.ds(jnp.minimum(row + 1, virt_ref.shape[0] - 1), 1), :]
            joined = jnp.where(lane < TILE, pltpu.roll(here, TILE, 1), pltpu.roll(after, TILE, 1))
            odd = lax.rem(me * home_tiles, 2)
            here = jnp.where(jnp.broadcast_to(odd == 1, here.shape), joined, here)
        pieces.append(here)
    pair_row = first_virt + jnp.concatenate(pieces, axis=1)

    def arrival(peer, part):
        return pltpu.make_async_remote_copy(
            src_ref=send.at[peer, :, parts[part]],
            dst_ref=recv.at[peer, :, parts[part]],
            send_sem=send_sems.at[part, peer],
            recv_sem=recv_sems.at[part, peer],
            device_id=(peer, my_sum),
            device_id_type=MESH,
        )

    reach = n_pair // 2
    half_rows = reach * rows
    halves = (flip, 1 - flip)

    def take_half(phase):
        def take_step(step, carry):
            first = halves[phase] * reach + 2 * step
            for side in range(2):
                peer = first + side
                mine = jnp.logical_not(at_end) & (peer == partner)

                @pl.when((peer != me) & jnp.logical_not(mine))
                def _():
                    arrival(peer, 0).wait_recv()

            both = recv[pl.ds(first, 2), :, :pick_cols].astype(F32).reshape(2 * rows, pick_cols)
            at = pl.multiple_of(step * 2 * rows, 2 * rows)
            left[phase, pl.ds(at, 2 * rows), :] = both.astype(BF16)
            return carry

        lax.fori_loop(0, reach // 2, take_step, 0)

    def part_of(phase, dest):
        terms = []
        for quad in range(quads):
            right = weights[dest, quad].reshape(need * TILE, 256)
            terms.append(jnp.dot(left[phase], right, preferred_element_type=F32))
        return jnp.concatenate(terms, axis=1).astype(BF16)

    def part_copy(phase, source, target):
        return pltpu.make_async_remote_copy(
            src_ref=part_send.at[phase, target],
            dst_ref=part_recv.at[phase, source],
            send_sem=part_send_sems.at[phase, target],
            recv_sem=part_recv_sems.at[phase, source],
            device_id=(me, target),
            device_id_type=MESH,
        )

    def other_sums():
        return [lax.rem(my_sum + step, n_sum) for step in range(1, n_sum)]

    take_half(0)
    for dest in other_sums():
        part_send[0, dest] = part_of(0, dest)

        @pl.when(dest > my_sum)
        def _():
            pl.semaphore_wait(ready_sum.at[dest], 1)

        part_copy(0, my_sum, dest).start()
    own_part[...] = part_of(0, my_sum)

    take_half(1)
    for dest in other_sums():
        part_send[1, dest] = part_of(1, dest)
        part_copy(1, my_sum, dest).start()
    def home_take(peer, carry):
        mine = jnp.logical_not(at_end) & (peer == partner)

        @pl.when((peer != me) & jnp.logical_not(mine))
        def _():
            arrival(peer, 1).wait_recv()

        return carry

    own_parts = (own_part[...], part_of(1, my_sum))
    lax.fori_loop(0, n_pair, home_take, 0)
    home = recv[:, :, pick_cols : pick_cols + home_pad].astype(F32).reshape(slab, home_pad)
    home = home.astype(BF16)

    def row_take(step, carry):
        row_arrival(lax.rem(column + step, width)).wait_recv()
        return carry

    lax.fori_loop(1, width, row_take, 0)
    totals = []
    for phase in range(2):
        own = own_parts[phase]
        lines = pl.ds(halves[phase] * reach, reach)
        here = recv[lines, :, pick_cols : pick_cols + home_pad].astype(F32)
        hh_rows = hh_all[pl.ds(halves[phase] * (LAYERS // 2), LAYERS // 2)].astype(F32)
        occ_rows = jnp.where(flip == phase, occ_pair[:half_rows], occ_pair[half_rows:])
        total = (pair_row - occ_rows) * here.reshape(half_rows, home_pad)
        total = total + jnp.dot(
            hh_rows.reshape(half_rows, slab).astype(BF16), home, preferred_element_type=F32
        )
        totals.append(total + own.astype(F32))
    for phase in range(2):
        total = totals[phase]
        for dest in other_sums():
            part_copy(phase, dest, dest).wait()
            total = total + part_recv[phase, dest].astype(F32)
        if out_ref.shape[1] == LANES:
            lines = home_cols // LANES
            base = halves[phase] * (half_rows * lines)
            for at in range(lines):
                out_ref[pl.ds(base + at, half_rows, stride=lines), :] = total[
                    :, at * LANES : (at + 1) * LANES
                ]
        else:
            base = pl.multiple_of(halves[phase] * half_rows, half_rows)
            out_ref[pl.ds(base, half_rows), :] = total[:, :home_cols]

    def sent_step(step, carry):
        block_copy(peer_at(step), 0).wait_send()
        block_copy(peer_at(step), 1).wait_send()
        return carry

    lax.fori_loop(0, directs, sent_step, 0)

    def row_sent(step, carry):
        row_copy(lax.rem(column + step, width)).wait_send()
        return carry

    lax.fori_loop(1, width, row_sent, 0)

    @pl.when(at_end)
    def _():
        column_copy((1 + flip) * width + column).wait_send()

    @pl.when(jnp.logical_not(at_end))
    def _():
        column_relay().wait_send()

        def column_sent(target, carry):
            @pl.when(target != layer)
            def _():
                column_copy(target * width + column).wait_send()

            return carry

        lax.fori_loop(0, LAYERS, column_sent, 0)

    def relayed_step(step, carry):
        peer = relay_peer(step)

        @pl.when(peer != me)
        def _():
            relay_copy(peer, 0).wait_send()
            relay_copy(peer, 1).wait_send()

        return carry

    @pl.when(jnp.logical_not(at_end))
    def _():
        lax.fori_loop(0, n_pair // 2, relayed_step, 0)

    @pl.when(at_end)
    def _():
        for copy in shard_copies():
            copy.wait_send()


def body(
    amps,
    amp_mask,
    hh_ints,
    integrals,
    slot_info,
    slot_count,
    need_tiles,
    slab_pairs,
    occ_energy,
    virt_energy,
):
    n_pair = lax.axis_size("pair")
    n_sum = lax.axis_size("sum")
    rows = amps.shape[0]
    cols = amps.shape[2]
    chunks = cols // LANES
    home_cols = cols // n_pair
    home_tiles = home_cols // TILE
    need = need_tiles.shape[2]
    owned, group = slot_info.shape[2], slot_info.shape[3]
    slab = rows * n_pair
    virt = virt_energy.shape[0]
    assert home_cols % TILE == 0 and virt % home_cols == 0 and cols % LANES == 0
    assert home_tiles % 4 == 0 or home_tiles < 4
    quads = -(-home_tiles // 4)
    home_pad = quads * 256
    block_cols = need * TILE + home_pad

    out_shape = (slab, home_cols) if home_cols % LANES else (slab * home_cols // LANES, LANES)

    vmem = pl.BlockSpec(memory_space=pltpu.VMEM)
    anywhere = pl.BlockSpec(memory_space=pltpu.HBM)
    dims = (n_pair, n_sum, rows, chunks, need, group, home_tiles, quads)
    residual = pl.pallas_call(
        functools.partial(ladder_kernel, dims),
        out_shape=pltpu.VMEM(out_shape, F32),
        in_specs=[anywhere] * 10,
        out_specs=vmem,
        scratch_shapes=[
            pltpu.SMEM(amp_mask.shape, I32),
            pltpu.SMEM((n_pair, need), I32),
            pltpu.VMEM((rows, cols), BF16),
            pltpu.VMEM(hh_ints.shape, BF16),
            pltpu.VMEM((group, owned), I32),
            pltpu.VMEM((1, owned), I32),
            pltpu.VMEM((2, slab), I32),
            pltpu.VMEM((1, occ_energy.shape[0]), F32),
            pltpu.VMEM((virt // LANES, LANES), F32),
            pltpu.VMEM((owned, 16 * group), F32),
            pltpu.VMEM((2, chunks, rows, LANES), F32),
            pltpu.VMEM((2, 2 * chunks, rows, LANES), F32),
            pltpu.VMEM((2, 2 * chunks, rows, LANES), F32),
            pltpu.VMEM((need * 16, 16 * group), F32),
            pltpu.VMEM((owned * group, TILE * TILE), BF16),
            pltpu.VMEM((n_sum, quads, need, 4, 16, 256), BF16),
            pltpu.VMEM((n_pair, rows, block_cols), BF16),
            pltpu.VMEM((n_pair, rows, block_cols), BF16),
            pltpu.VMEM((2, slab // 2, need * TILE), BF16),
            pltpu.VMEM((slab // 2, home_pad), BF16),
            pltpu.VMEM((2, n_sum, slab // 2, home_pad), BF16),
            pltpu.VMEM((2, n_sum, slab // 2, home_pad), BF16),
            pltpu.VMEM((rows, cols), BF16),
            pltpu.VMEM((rows, slab), BF16),
            pltpu.VMEM((LAYERS, n_pair // LAYERS, rows, slab), BF16),
            pltpu.VMEM((n_pair // 2, rows, block_cols), BF16),
            pltpu.SemaphoreType.REGULAR((n_pair,)),
            pltpu.SemaphoreType.REGULAR((n_sum,)),
            pltpu.SemaphoreType.DMA((10,)),
            pltpu.SemaphoreType.DMA((2, n_pair)),
            pltpu.SemaphoreType.DMA((2, n_pair)),
            pltpu.SemaphoreType.DMA((2, n_sum)),
            pltpu.SemaphoreType.DMA((2, n_sum)),
            pltpu.SemaphoreType.DMA((3,)),
            pltpu.SemaphoreType.DMA((3,)),
            pltpu.SemaphoreType.DMA((2, n_pair // 2)),
            pltpu.SemaphoreType.DMA((LAYERS,)),
            pltpu.SemaphoreType.DMA((LAYERS,)),
            pltpu.SemaphoreType.DMA((n_pair // LAYERS,)),
            pltpu.SemaphoreType.DMA((n_pair // LAYERS,)),
        ],
        compiler_params=pltpu.CompilerParams(
            collective_id=0, has_side_effects=True, vmem_limit_bytes=56 * 1024 * 1024
        ),
    )(
        amp_mask,
        need_tiles.reshape(n_pair, need),
        amps.reshape(rows, cols),
        hh_ints,
        slot_info.reshape(owned, group).T,
        slot_count.reshape(1, owned),
        slab_pairs.T,
        occ_energy.reshape(1, -1),
        virt_energy.reshape(virt // LANES, LANES),
        integrals.reshape(owned * group, TILE * TILE),
    )
    return residual.reshape(slab, 1, home_cols)


def solution(mesh):
    return jax.shard_map(
        body,
        mesh=mesh,
        in_specs=(
            P("pair", "sum", None),
            P("sum", None),
            P("pair", None),
            P("pair", "sum", None, None),
            P("pair", "sum", None, None),
            P("pair", "sum", None),
            P(None, "sum", None),
            P(),
            P(),
            P(),
        ),
        out_specs=P(None, "sum", "pair"),
        check_vma=False,
    )
```

```python
import functools

import jax
import jax.numpy as jnp
from jax import lax
from jax.experimental import pallas as pl
from jax.experimental.pallas import tpu as pltpu
from jax.sharding import PartitionSpec as P

TILE = 64
LANES = 128
LAYERS = 4
EARLY = 0
MESH = pl.DeviceIdType.MESH
BF16 = jnp.bfloat16
F32 = jnp.float32
I32 = jnp.int32


def iota(shape, axis):
    return lax.broadcasted_iota(I32, shape, axis)


def ladder_kernel(
    dims,
    mask_in,
    need_in,
    amps_in,
    hh_in,
    info_in,
    count_in,
    slab_in,
    occ_in,
    virt_in,
    ints_in,
    out_ref,
    mask_ref,
    need_ref,
    amps_ref,
    hh_ref,
    info_ref,
    count_ref,
    slab_ref,
    occ_ref,
    virt_ref,
    pos_ref,
    plain,
    low,
    high,
    pattern,
    ints,
    weights,
    send,
    recv,
    left,
    own_part,
    part_send,
    part_recv,
    shard_ref,
    shard_hh,
    hh_all,
    relay,
    ready,
    ready_sum,
    in_sems,
    send_sems,
    recv_sems,
    part_send_sems,
    part_recv_sems,
    shard_send_sems,
    shard_recv_sems,
    relay_sems,
    column_send_sems,
    column_recv_sems,
    row_send_sems,
    row_recv_sems,
):
    n_pair, n_sum, rows, chunks, need, group, home_tiles, quads = dims
    slab = rows * n_pair
    home_pad = quads * 256
    home_cols = home_tiles * TILE
    pick_cols = need * TILE
    me = lax.axis_index("pair")
    my_sum = lax.axis_index("sum")

    width = n_pair // LAYERS
    layer, column = me // width, lax.rem(me, width)
    flip = layer // 2
    at_end = layer == flip * (LAYERS - 1)
    partner = lax.rem(me + n_pair // 2, n_pair)

    barrier = pltpu.get_barrier_semaphore()

    def greet(peer, carry):
        pl.semaphore_signal(barrier, inc=1, device_id=(peer, my_sum), device_id_type=MESH)
        return carry

    def greet_sum(peer, carry):
        pl.semaphore_signal(barrier, inc=1, device_id=(me, peer), device_id_type=MESH)
        return carry

    pairs_of_refs = (
        (mask_in, mask_ref),
        (amps_in, amps_ref),
        (need_in, need_ref),
        (hh_in, hh_ref),
        (info_in, info_ref),
        (count_in, count_ref),
        (slab_in, slab_ref),
        (occ_in, occ_ref),
        (virt_in, virt_ref),
        (ints_in, ints),
    )
    fetches = [
        pltpu.make_async_copy(src, dst, in_sems.at[at]) for at, (src, dst) in enumerate(pairs_of_refs)
    ]
    for fetch in fetches:
        fetch.start()
    lax.fori_loop(me + 1, n_pair, greet, 0)
    lax.fori_loop(my_sum + 1, n_sum, greet_sum, 0)

    @pl.when(me + my_sum > 0)
    def _():
        pl.semaphore_wait(barrier, me + my_sum)

    split = 2 * chunks // 3
    head, rest = slice(0, split * LANES), slice(split * LANES, chunks * LANES)
    shard_parts = (
        (hh_in, shard_hh),
        (amps_in.at[:, head], shard_ref.at[:, head]),
        (amps_in.at[:, rest], shard_ref.at[:, rest]),
    )

    def shard_copies():
        return [
            pltpu.make_async_remote_copy(
                src_ref=src,
                dst_ref=dst,
                send_sem=shard_send_sems.at[at],
                recv_sem=shard_recv_sems.at[at],
                device_id=(partner, my_sum),
                device_id_type=MESH,
            )
            for at, (src, dst) in enumerate(shard_parts)
        ]

    @pl.when(at_end & (flip == 1))
    def _():
        for copy in shard_copies():
            copy.start()

    def answer(peer, carry):
        @pl.when((peer >= width) | (flip == 0) | (peer == partner))
        def _():
            pl.semaphore_signal(
                ready.at[me], inc=1, device_id=(peer, my_sum), device_id_type=MESH
            )

        return carry

    def answer_sum(peer, carry):
        pl.semaphore_signal(
            ready_sum.at[my_sum], inc=1, device_id=(me, peer), device_id_type=MESH
        )
        return carry

    lax.fori_loop(0, me, answer, 0)
    lax.fori_loop(0, my_sum, answer_sum, 0)

    def wait_ready(peer):
        @pl.when(peer > me)
        def _():
            pl.semaphore_wait(ready.at[peer], 1)

    fetches[0].wait()
    fetches[1].wait()

    low_half = iota((rows, LANES), 1) < TILE
    row_at = iota((LANES, LANES), 0)
    col_at = iota((LANES, LANES), 1)
    origin = (
        (col_at & 64) + (col_at & 32) + ((col_at & 15) << 1) + ((col_at >> 4) & 1)
    )
    shuffle = jnp.where(row_at == origin, 1.0, 0.0).astype(BF16)

    def unfold(which, source, first, last):
        for chunk in range(first, last):
            keep = jnp.where(low_half, mask_ref[0, 2 * chunk], mask_ref[0, 2 * chunk + 1]).astype(F32)
            values = source[:, chunk * LANES : (chunk + 1) * LANES].astype(F32)
            plain[which, chunk] = values * keep
        moved = jnp.dot(
            plain[which, first:last].reshape((last - first) * rows, LANES).astype(BF16),
            shuffle,
            preferred_element_type=F32,
        )
        turned = pltpu.roll(moved, TILE, 1)
        count = last - first
        moved = moved.reshape(count, rows, LANES)
        turned = turned.reshape(count, rows, LANES)
        tiles = slice(2 * first, 2 * last)
        low[which, tiles] = jnp.stack([moved, turned], axis=1).reshape(2 * count, rows, LANES)
        high[which, tiles] = jnp.stack([turned, moved], axis=1).reshape(2 * count, rows, LANES)

    unfold(0, amps_ref, 0, chunks)

    fetches[2].wait()
    fetches[3].wait()

    def pack(which, peer):
        pieces = []
        for at in range(need // 2):
            first = need_ref[peer, 2 * at]
            second = need_ref[peer, 2 * at + 1]
            pieces.append(jnp.where(low_half, low[which, first], high[which, second]))
        for at in range(home_pad // LANES):
            if home_tiles % 2 == 0:
                pieces.append(plain[which, peer * (home_tiles // 2) + at])
            else:
                first = peer * home_tiles + 2 * at
                odd = lax.rem(first, 2)
                chunk = first // 2
                after = jnp.minimum(chunk + 1, chunks - 1)
                here = plain[which, chunk]
                joined = jnp.where(
                    low_half, pltpu.roll(here, TILE, 1), pltpu.roll(plain[which, after], TILE, 1)
                )
                pieces.append(jnp.where(jnp.broadcast_to(odd == 1, here.shape), joined, here))
        return jnp.concatenate(pieces, axis=1).astype(BF16)

    def place(to_layer, turn):
        ahead = jnp.where(turn == 0, 0, 1 + lax.rem(column + turn + width - 2, width - 1))
        beside = lax.rem(column + turn + jnp.where(to_layer == layer, 1, 0), width)
        return to_layer * width + jnp.where(to_layer == 0, ahead, beside)

    def peer_at(step):
        own = width - 1
        low_step, high_step = step - width - own, step - 2 * width
        up_layer = jnp.where((low_step >= 1) & (low_step < width + 1), 3, 2)
        up_turn = jnp.where(low_step < 1, low_step, jnp.where(up_layer == 3, low_step - 1, low_step - width))
        low_layer = jnp.where(step < width, 0, jnp.where(low_step < 0, 1, up_layer))
        low_turn = jnp.where(step < width, step, jnp.where(low_step < 0, step - width, up_turn))
        high_layer = jnp.where(high_step < 0, step // width, jnp.where(high_step < own, 2, 3))
        high_turn = jnp.where(
            high_step < 0, lax.rem(step, width), jnp.where(high_step < own, high_step, high_step - own)
        )
        end_layer = jnp.where(step < own, layer, 1 + flip)
        end_turn = jnp.where(step < own, step, step - own)
        to_layer = jnp.where(at_end, end_layer, jnp.where(flip == 0, low_layer, high_layer))
        turn = jnp.where(at_end, end_turn, jnp.where(flip == 0, low_turn, high_turn))
        own_place = layer * width + lax.rem(column + turn + 1, width)
        return jnp.where(to_layer == layer, own_place, place(to_layer, turn))

    parts = (slice(0, pick_cols), slice(pick_cols, pick_cols + home_pad))

    def split_home(peer):
        return peer != 0

    def block_copy(peer, part):
        return pltpu.make_async_remote_copy(
            src_ref=send.at[peer, :, parts[part]],
            dst_ref=recv.at[me, :, parts[part]],
            send_sem=send_sems.at[part, peer],
            recv_sem=recv_sems.at[part, me],
            device_id=(peer, my_sum),
            device_id_type=MESH,
        )

    def column_copy(peer):
        return pltpu.make_async_remote_copy(
            src_ref=hh_ref,
            dst_ref=hh_all.at[layer, column],
            send_sem=column_send_sems.at[peer // width],
            recv_sem=column_recv_sems.at[layer],
            device_id=(peer, my_sum),
            device_id_type=MESH,
        )

    far_layer = partner // width

    def column_relay():
        return pltpu.make_async_remote_copy(
            src_ref=shard_hh,
            dst_ref=hh_all.at[far_layer, column],
            send_sem=column_send_sems.at[layer],
            recv_sem=column_recv_sems.at[far_layer],
            device_id=(flip * (LAYERS - 1) * width + column, my_sum),
            device_id_type=MESH,
        )

    def row_copy(place):
        return pltpu.make_async_remote_copy(
            src_ref=hh_all.at[:, column],
            dst_ref=hh_all.at[:, column],
            send_sem=row_send_sems.at[place],
            recv_sem=row_recv_sems.at[column],
            device_id=(layer * width + place, my_sum),
            device_id_type=MESH,
        )

    def column_arrival(source):
        return pltpu.make_async_remote_copy(
            src_ref=hh_ref,
            dst_ref=hh_all.at[source, column],
            send_sem=column_send_sems.at[source],
            recv_sem=column_recv_sems.at[source],
            device_id=(source * width + column, my_sum),
            device_id_type=MESH,
        )

    def row_arrival(place):
        return pltpu.make_async_remote_copy(
            src_ref=hh_all.at[:, place],
            dst_ref=hh_all.at[:, place],
            send_sem=row_send_sems.at[place],
            recv_sem=row_recv_sems.at[place],
            device_id=(layer * width + place, my_sum),
            device_id_type=MESH,
        )

    hh_all[layer, column] = hh_ref[...]

    def send_step(step, carry):
        peer = peer_at(step)
        send[peer] = pack(0, peer)
        wait_ready(peer)
        block_copy(peer, 0).start()

        @pl.when(jnp.logical_not(split_home(peer)))
        def _():
            block_copy(peer, 1).start()

        @pl.when(lax.rem(peer, width) == column)
        def _():
            column_copy(peer).start()

        @pl.when(at_end & (flip == 0) & (step == width - 2 + EARLY))
        def _():
            wait_ready(partner)
            for copy in shard_copies():
                copy.start()

        return carry

    directs = jnp.where(at_end, n_pair // 2 - 1, n_pair - 1)
    later = jnp.where(flip == 0, 2 * width - 1, 0)
    soon = jnp.where(at_end, directs, directs - later)
    lax.fori_loop(0, soon, send_step, 0)
    recv[me] = pack(0, me)

    spread_rows = need * 16
    spread_cols = 16 * group
    row_at = iota((spread_rows, spread_cols), 0)
    col_at = iota((spread_rows, spread_cols), 1)
    pattern[...] = jnp.where((row_at & 15) == col_at // group, row_at >> 4, -1).astype(F32)
    pair_low = iota((spread_rows, LANES), 1) < TILE
    for fetch in fetches[4:]:
        fetch.wait()
    live = iota(info_ref.shape, 0) < count_ref[...]
    positions = jnp.where(live, info_ref[...], -2).astype(F32).astype(BF16)
    repeat = jnp.where(
        iota((group, spread_cols), 0) == lax.rem(iota((group, spread_cols), 1), group), 1.0, 0.0
    ).astype(BF16)
    pos_ref[...] = lax.dot_general(
        positions, repeat, (((0,), (0,)), ((), ())), preferred_element_type=F32
    )

    def spread(tile):
        picked = jnp.where(pattern[...] == pos_ref[pl.ds(tile, 1), :], 1.0, 0.0).astype(BF16)
        base = pl.multiple_of(tile * group, group)
        halves = []
        for half in range(2):
            stack = [
                ints[pl.ds(base, group), (half * 16 + k) * LANES : (half * 16 + k + 1) * LANES]
                for k in range(16)
            ]
            halves.append(jnp.concatenate(stack, axis=0))
        stacked = jnp.concatenate(halves, axis=1)
        return jnp.dot(picked, stacked, preferred_element_type=F32)

    def spread_quad(at, carry):
        dest = at // quads
        quad = lax.rem(at, quads)
        first = dest * home_tiles + quad * 4
        for pair in range(2):
            lone = quads == 1 and 2 * pair + 1 >= home_tiles
            a = spread(first + 2 * pair)
            b = None if lone else spread(first + 2 * pair + 1)
            for half in range(2):
                a_half = a[:, half * LANES : (half + 1) * LANES]
                b_half = jnp.zeros_like(a_half) if lone else b[:, half * LANES : (half + 1) * LANES]
                even = jnp.where(pair_low, a_half, pltpu.roll(b_half, TILE, 1)).astype(BF16)
                odd = jnp.where(pair_low, pltpu.roll(a_half, TILE, 1), b_half).astype(BF16)
                cols = slice(pair * LANES, (pair + 1) * LANES)
                weights[dest, quad, :, 2 * half, :, cols] = even.reshape(need, 16, LANES)
                weights[dest, quad, :, 2 * half + 1, :, cols] = odd.reshape(need, 16, LANES)
        return carry


    some = n_sum * quads // 2
    lax.fori_loop(0, some, spread_quad, 0)
    lax.fori_loop(soon, directs, send_step, 0)

    def home_step(step, carry):
        @pl.when(split_home(peer_at(step)))
        def _():
            block_copy(peer_at(step), 1).start()

        return carry

    lax.fori_loop(0, directs, home_step, 0)
    lax.fori_loop(some, n_sum * quads, spread_quad, 0)

    def relay_copy(peer, part):
        slot = lax.rem(peer, n_pair // 2)
        return pltpu.make_async_remote_copy(
            src_ref=relay.at[slot, :, parts[part]],
            dst_ref=recv.at[partner, :, parts[part]],
            send_sem=relay_sems.at[part, slot],
            recv_sem=recv_sems.at[part, partner],
            device_id=(peer, my_sum),
            device_id_type=MESH,
        )

    def relay_peer(step):
        turn = lax.rem(step, 2)
        near = jnp.where(flip == 0, turn, 1 - turn)
        return place(flip * 2 + near, step // 2)

    @pl.when(jnp.logical_not(at_end))
    def _():
        copies = shard_copies()
        copies[0].wait_recv()
        hh_all[far_layer, column] = shard_hh[...]
        column_relay().start()
        copies[1].wait_recv()
        unfold(1, shard_ref, 0, split)
        copies[2].wait_recv()
        unfold(1, shard_ref, split, chunks)

        def relay_step(step, carry):
            peer = relay_peer(step)
            block = pack(1, peer)

            @pl.when(peer == me)
            def _():
                recv[partner] = block

            @pl.when(peer != me)
            def _():
                relay[lax.rem(peer, n_pair // 2)] = block
                relay_copy(peer, 0).start()

            @pl.when((peer != me) & (peer == 0))
            def _():
                relay_copy(peer, 1).start()

            return carry

        lax.fori_loop(0, n_pair // 2, relay_step, 0)

        def relay_home_step(step, carry):
            peer = relay_peer(step)

            @pl.when((peer != me) & jnp.logical_not(peer == 0))
            def _():
                relay_copy(peer, 1).start()

            return carry

        lax.fori_loop(0, n_pair // 2, relay_home_step, 0)

    def column_step(source, carry):
        @pl.when((source != layer) & (at_end | (source != far_layer_of_end)))
        def _():
            column_arrival(source).wait_recv()

        return carry

    def row_step(step, carry):
        row_copy(lax.rem(column + step, width)).start()
        return carry

    far_layer_of_end = (1 - flip) * (LAYERS - 1)
    lax.fori_loop(0, LAYERS, column_step, 0)
    lax.fori_loop(1, width, row_step, 0)

    occ_at = iota((slab, occ_ref.shape[1]), 1).astype(F32)
    occ_row = occ_ref[...]
    orbitals = jnp.concatenate([slab_ref[...].astype(F32), jnp.zeros((6, slab), F32)], axis=0).T
    occ_i = jnp.sum(jnp.where(orbitals[:, 0:1] == occ_at, occ_row, 0.0), axis=1, keepdims=True)
    occ_j = jnp.sum(jnp.where(orbitals[:, 1:2] == occ_at, occ_row, 0.0), axis=1, keepdims=True)
    occ_pair = occ_i + occ_j

    virt_count = virt_ref.shape[0] * LANES
    start = me * home_cols
    first_at = my_sum * (chunks * LANES // virt_count) + start // virt_count
    lane = iota((1, LANES), 1)
    first_virt = jnp.sum(
        jnp.where(lane == lax.rem(first_at, LANES), virt_ref[pl.ds(first_at // LANES, 1), :], 0.0),
        axis=1,
        keepdims=True,
    )
    pieces = []
    for at in range(home_pad // LANES):
        row = (lax.rem(start, virt_count) + at * LANES) // LANES
        here = virt_ref[pl.ds(row, 1), :]
        if home_tiles % 2:
            after = virt_ref[pl.ds(jnp.minimum(row + 1, virt_ref.shape[0] - 1), 1), :]
            joined = jnp.where(lane < TILE, pltpu.roll(here, TILE, 1), pltpu.roll(after, TILE, 1))
            odd = lax.rem(me * home_tiles, 2)
            here = jnp.where(jnp.broadcast_to(odd == 1, here.shape), joined, here)
        pieces.append(here)
    pair_row = first_virt + jnp.concatenate(pieces, axis=1)

    def arrival(peer, part):
        return pltpu.make_async_remote_copy(
            src_ref=send.at[peer, :, parts[part]],
            dst_ref=recv.at[peer, :, parts[part]],
            send_sem=send_sems.at[part, peer],
            recv_sem=recv_sems.at[part, peer],
            device_id=(peer, my_sum),
            device_id_type=MESH,
        )

    reach = n_pair // 2
    half_rows = reach * rows
    halves = (flip, 1 - flip)

    def take_half(phase):
        def take_step(step, carry):
            first = halves[phase] * reach + 2 * step
            for side in range(2):
                peer = first + side
                mine = jnp.logical_not(at_end) & (peer == partner)

                @pl.when((peer != me) & jnp.logical_not(mine))
                def _():
                    arrival(peer, 0).wait_recv()

            both = recv[pl.ds(first, 2), :, :pick_cols].astype(F32).reshape(2 * rows, pick_cols)
            at = pl.multiple_of(step * 2 * rows, 2 * rows)
            left[phase, pl.ds(at, 2 * rows), :] = both.astype(BF16)
            return carry

        lax.fori_loop(0, reach // 2, take_step, 0)

    def part_of(phase, dest):
        terms = []
        for quad in range(quads):
            right = weights[dest, quad].reshape(need * TILE, 256)
            terms.append(jnp.dot(left[phase], right, preferred_element_type=F32))
        return jnp.concatenate(terms, axis=1).astype(BF16)

    def part_copy(phase, source, target):
        return pltpu.make_async_remote_copy(
            src_ref=part_send.at[phase, target],
            dst_ref=part_recv.at[phase, source],
            send_sem=part_send_sems.at[phase, target],
            recv_sem=part_recv_sems.at[phase, source],
            device_id=(me, target),
            device_id_type=MESH,
        )

    def other_sums():
        return [lax.rem(my_sum + step, n_sum) for step in range(1, n_sum)]

    take_half(0)
    for dest in other_sums():
        part_send[0, dest] = part_of(0, dest)

        @pl.when(dest > my_sum)
        def _():
            pl.semaphore_wait(ready_sum.at[dest], 1)

        part_copy(0, my_sum, dest).start()
    own_part[...] = part_of(0, my_sum)

    take_half(1)
    for dest in other_sums():
        part_send[1, dest] = part_of(1, dest)
        part_copy(1, my_sum, dest).start()
    def home_take(peer, carry):
        mine = jnp.logical_not(at_end) & (peer == partner)

        @pl.when((peer != me) & jnp.logical_not(mine))
        def _():
            arrival(peer, 1).wait_recv()

        return carry

    own_parts = (own_part[...], part_of(1, my_sum))
    lax.fori_loop(0, n_pair, home_take, 0)
    home = recv[:, :, pick_cols : pick_cols + home_pad].astype(F32).reshape(slab, home_pad)
    home = home.astype(BF16)

    def row_take(step, carry):
        row_arrival(lax.rem(column + step, width)).wait_recv()
        return carry

    lax.fori_loop(1, width, row_take, 0)
    totals = []
    for phase in range(2):
        own = own_parts[phase]
        lines = pl.ds(halves[phase] * reach, reach)
        here = recv[lines, :, pick_cols : pick_cols + home_pad].astype(F32)
        hh_rows = hh_all[pl.ds(halves[phase] * (LAYERS // 2), LAYERS // 2)].astype(F32)
        occ_rows = jnp.where(flip == phase, occ_pair[:half_rows], occ_pair[half_rows:])
        total = (pair_row - occ_rows) * here.reshape(half_rows, home_pad)
        total = total + jnp.dot(
            hh_rows.reshape(half_rows, slab).astype(BF16), home, preferred_element_type=F32
        )
        totals.append(total + own.astype(F32))
    for phase in range(2):
        total = totals[phase]
        for dest in other_sums():
            part_copy(phase, dest, dest).wait()
            total = total + part_recv[phase, dest].astype(F32)
        if out_ref.shape[1] == LANES:
            lines = home_cols // LANES
            base = halves[phase] * (half_rows * lines)
            for at in range(lines):
                out_ref[pl.ds(base + at, half_rows, stride=lines), :] = total[
                    :, at * LANES : (at + 1) * LANES
                ]
        else:
            base = pl.multiple_of(halves[phase] * half_rows, half_rows)
            out_ref[pl.ds(base, half_rows), :] = total[:, :home_cols]

    def sent_step(step, carry):
        block_copy(peer_at(step), 0).wait_send()
        block_copy(peer_at(step), 1).wait_send()
        return carry

    lax.fori_loop(0, directs, sent_step, 0)

    def row_sent(step, carry):
        row_copy(lax.rem(column + step, width)).wait_send()
        return carry

    lax.fori_loop(1, width, row_sent, 0)

    @pl.when(at_end)
    def _():
        column_copy((1 + flip) * width + column).wait_send()

    @pl.when(jnp.logical_not(at_end))
    def _():
        column_relay().wait_send()

        def column_sent(target, carry):
            @pl.when(target != layer)
            def _():
                column_copy(target * width + column).wait_send()

            return carry

        lax.fori_loop(0, LAYERS, column_sent, 0)

    def relayed_step(step, carry):
        peer = relay_peer(step)

        @pl.when(peer != me)
        def _():
            relay_copy(peer, 0).wait_send()
            relay_copy(peer, 1).wait_send()

        return carry

    @pl.when(jnp.logical_not(at_end))
    def _():
        lax.fori_loop(0, n_pair // 2, relayed_step, 0)

    @pl.when(at_end)
    def _():
        for copy in shard_copies():
            copy.wait_send()


def body(
    amps,
    amp_mask,
    hh_ints,
    integrals,
    slot_info,
    slot_count,
    need_tiles,
    slab_pairs,
    occ_energy,
    virt_energy,
):
    n_pair = lax.axis_size("pair")
    n_sum = lax.axis_size("sum")
    rows = amps.shape[0]
    cols = amps.shape[2]
    chunks = cols // LANES
    home_cols = cols // n_pair
    home_tiles = home_cols // TILE
    need = need_tiles.shape[2]
    owned, group = slot_info.shape[2], slot_info.shape[3]
    slab = rows * n_pair
    virt = virt_energy.shape[0]
    assert home_cols % TILE == 0 and virt % home_cols == 0 and cols % LANES == 0
    assert home_tiles % 4 == 0 or home_tiles < 4
    quads = -(-home_tiles // 4)
    home_pad = quads * 256
    block_cols = need * TILE + home_pad

    out_shape = (slab, home_cols) if home_cols % LANES else (slab * home_cols // LANES, LANES)

    vmem = pl.BlockSpec(memory_space=pltpu.VMEM)
    anywhere = pl.BlockSpec(memory_space=pltpu.HBM)
    dims = (n_pair, n_sum, rows, chunks, need, group, home_tiles, quads)
    residual = pl.pallas_call(
        functools.partial(ladder_kernel, dims),
        out_shape=pltpu.VMEM(out_shape, F32),
        in_specs=[anywhere] * 10,
        out_specs=vmem,
        scratch_shapes=[
            pltpu.SMEM(amp_mask.shape, I32),
            pltpu.SMEM((n_pair, need), I32),
            pltpu.VMEM((rows, cols), BF16),
            pltpu.VMEM(hh_ints.shape, BF16),
            pltpu.VMEM((group, owned), I32),
            pltpu.VMEM((1, owned), I32),
            pltpu.VMEM((2, slab), I32),
            pltpu.VMEM((1, occ_energy.shape[0]), F32),
            pltpu.VMEM((virt // LANES, LANES), F32),
            pltpu.VMEM((owned, 16 * group), F32),
            pltpu.VMEM((2, chunks, rows, LANES), F32),
            pltpu.VMEM((2, 2 * chunks, rows, LANES), F32),
            pltpu.VMEM((2, 2 * chunks, rows, LANES), F32),
            pltpu.VMEM((need * 16, 16 * group), F32),
            pltpu.VMEM((owned * group, TILE * TILE), BF16),
            pltpu.VMEM((n_sum, quads, need, 4, 16, 256), BF16),
            pltpu.VMEM((n_pair, rows, block_cols), BF16),
            pltpu.VMEM((n_pair, rows, block_cols), BF16),
            pltpu.VMEM((2, slab // 2, need * TILE), BF16),
            pltpu.VMEM((slab // 2, home_pad), BF16),
            pltpu.VMEM((2, n_sum, slab // 2, home_pad), BF16),
            pltpu.VMEM((2, n_sum, slab // 2, home_pad), BF16),
            pltpu.VMEM((rows, cols), BF16),
            pltpu.VMEM((rows, slab), BF16),
            pltpu.VMEM((LAYERS, n_pair // LAYERS, rows, slab), BF16),
            pltpu.VMEM((n_pair // 2, rows, block_cols), BF16),
            pltpu.SemaphoreType.REGULAR((n_pair,)),
            pltpu.SemaphoreType.REGULAR((n_sum,)),
            pltpu.SemaphoreType.DMA((10,)),
            pltpu.SemaphoreType.DMA((2, n_pair)),
            pltpu.SemaphoreType.DMA((2, n_pair)),
            pltpu.SemaphoreType.DMA((2, n_sum)),
            pltpu.SemaphoreType.DMA((2, n_sum)),
            pltpu.SemaphoreType.DMA((3,)),
            pltpu.SemaphoreType.DMA((3,)),
            pltpu.SemaphoreType.DMA((2, n_pair // 2)),
            pltpu.SemaphoreType.DMA((LAYERS,)),
            pltpu.SemaphoreType.DMA((LAYERS,)),
            pltpu.SemaphoreType.DMA((n_pair // LAYERS,)),
            pltpu.SemaphoreType.DMA((n_pair // LAYERS,)),
        ],
        compiler_params=pltpu.CompilerParams(
            collective_id=0, has_side_effects=True, vmem_limit_bytes=56 * 1024 * 1024
        ),
    )(
        amp_mask,
        need_tiles.reshape(n_pair, need),
        amps.reshape(rows, cols),
        hh_ints,
        slot_info.reshape(owned, group).T,
        slot_count.reshape(1, owned),
        slab_pairs.T,
        occ_energy.reshape(1, -1),
        virt_energy.reshape(virt // LANES, LANES),
        integrals.reshape(owned * group, TILE * TILE),
    )
    return residual.reshape(slab, 1, home_cols)


def solution(mesh):
    return jax.shard_map(
        body,
        mesh=mesh,
        in_specs=(
            P("pair", "sum", None),
            P("sum", None),
            P("pair", None),
            P("pair", "sum", None, None),
            P("pair", "sum", None, None),
            P("pair", "sum", None),
            P(None, "sum", None),
            P(),
            P(),
            P(),
        ),
        out_specs=P(None, "sum", "pair"),
        check_vma=False,
    )
```
